32 devices in a mesh: group: 2 (over x), seq: 16 (over z, y, core).
Axes of the slice: x: 2, y: 2, z: 4, core: 2. Of those that a mesh axis runs over, the one named last changes fastest.
Arguments:
- tokens: bfloat16 [16384, 2048], P(('group', 'seq')), parts along dimension 0, may hold values from -6 to 6
- w_qkv: bfloat16 [2048, 3072], P('seq'), may hold values from -0.125 to 0.125
- w_out: bfloat16 [1024, 2048], P('seq'), may hold values from -0.1875 to 0.1875
- level_weight: float32 [14, 4, 16384], P(None, None, ('group', 'seq')), parts along dimension 2, may hold values from 0.1 to 1
Outputs:
- mixed: bfloat16 [16384, 2048], P(('group', 'seq')), parts along dimension 0
The draws below stay inside these ranges and needn't reach their ends.
There are 2 independent parts, one for each index of `group`. The reference program is written for one: setup_inputs(seed, part) draws one part's arguments, and reference() takes and returns one part's arrays. A program takes and returns all parts, laid end to end along the dimension named above; an argument that names none is the same for every part. Nothing has to cross between parts.
All inputs are finite; a program needn't handle non-finite values.
Results may differ from the reference program's by a relative error of at most 0.0085.
Values may be sent and summed in bfloat16 or wider, within the bound.
A program may use at most 128 MiB of HBM per device.

```python
import math
import jax
import jax.numpy as jnp
from jax import lax

D = 2048
HEADS = 4
HEAD = 256
SPAN = 256
TOKENS = 8192
NCHUNK = 32
CBITS = 8
NBITS = 5
LEVELS = 14


def level_of(stream_key, shape, split, smallest, top_value):
    factor_of, own = 1.0, jax.random.fold_in(stream_key, 6)
    for axis_at, parts in split:
        draws = jnp.exp(jax.random.uniform(jax.random.fold_in(own, axis_at), (parts,), jnp.float32, smallest / len(split), top_value / len(split)))
        factor_of = factor_of * jnp.repeat(draws, shape[axis_at] // parts).reshape([-1 if axis == axis_at else 1 for axis in range(len(shape))])
    return factor_of


def bell_draw(stream_key, shape, width, limit, split=(), held_as=jnp.bfloat16):
    factor_of = level_of(stream_key, shape, split, -0.22, 0.18) if split else 1.0
    entries = jax.random.normal(stream_key, shape, jnp.float32) * width * factor_of
    return jnp.minimum(jnp.maximum(entries, -limit), limit).astype(held_as)


def setup_inputs(seed: int = 0, part: int = 0) -> dict:
    seeds = jax.random.split(jax.random.key(seed), 5)
    own_keys = jax.random.split(jax.random.fold_in(seeds[4], part), 5)
    return {
        "tokens": bell_draw(own_keys[0], (TOKENS, D), 1.0, 6.0, ((0, 16),)),
        "w_qkv": bell_draw(seeds[1], (D, 3 * HEADS * HEAD), D ** -0.5, 0.125, ((0, 16),)),
        "w_out": bell_draw(seeds[2], (HEADS * HEAD, D), (HEADS * HEAD) ** -0.5, 0.1875, ((0, 16),)),
        "level_weight": jnp.clip(jnp.exp(math.log(1.0) - 2.3025851 * jax.random.uniform(own_keys[3], (LEVELS, HEADS, TOKENS), jnp.float32) ** level_of(own_keys[3], (LEVELS, HEADS, TOKENS), ((2, 16),), -0.2, 0.2)), 0.1, 1.0),
    }


def bit_length_of(values):
    result = jnp.zeros(values.shape, jnp.int32)
    for bit_pos in range(24):
        result = result + (values >= 1 << bit_pos).astype(jnp.int32)
    return result

def intra_table(span, cbits, head):
    position = jnp.arange(span, dtype=jnp.int32)
    pair_level = bit_length_of(position[:, None] ^ position[None, :])
    causal = position[:, None] >= position[None, :]
    levels_all = jnp.arange(cbits + 1, dtype=jnp.int32)
    gains = jnp.asarray([1.0 / math.sqrt(head * max(1, 2 ** (level_no - 1))) for level_no in range(cbits + 1)], jnp.float32)
    onehot = ((pair_level[None] == levels_all[:, None, None]) & causal[None]).astype(jnp.float32)
    return onehot * gains[:, None, None]

def reference(tokens, w_qkv, w_out, level_weight):
    highest = lax.Precision.HIGHEST
    head_cols = HEADS * HEAD
    qkv = jnp.dot(tokens, w_qkv, preferred_element_type=jnp.float32).astype(jnp.bfloat16)
    queries = qkv[:, :head_cols].reshape(NCHUNK, SPAN, HEADS, HEAD).astype(jnp.float32)
    key_rows = qkv[:, head_cols:2 * head_cols].reshape(NCHUNK, SPAN, HEADS, HEAD).astype(jnp.float32)
    value_rows = qkv[:, 2 * head_cols:].reshape(NCHUNK, SPAN, HEADS, HEAD).astype(jnp.float32)
    weights = level_weight.reshape(LEVELS, HEADS, NCHUNK, SPAN)
    table = intra_table(SPAN, CBITS, HEAD)
    mixing = jnp.einsum('lij,lhci->chij', table, weights[:CBITS + 1], precision=highest)
    scores = jnp.einsum('cihe,cjhe->chij', queries, key_rows, precision=highest)
    probs = (scores * mixing).astype(jnp.bfloat16)
    probs = lax.optimization_barrier(probs).astype(jnp.float32)
    intra = jnp.einsum('chij,cjhe->cihe', probs, value_rows, precision=highest)
    states = jnp.einsum('cjhe,cjhf->chef', key_rows, value_rows, precision=highest)
    inter = jnp.zeros((NCHUNK, SPAN, HEADS, HEAD), jnp.float32)
    for level_no in range(1, NBITS + 1):
        half_size = 2 ** (level_no - 1)
        blocks = NCHUNK // (2 * half_size)
        left = states.reshape(blocks, 2, half_size, HEADS, HEAD, HEAD)[:, 0].sum(axis=1)
        right_q = queries.reshape(blocks, 2, half_size, SPAN, HEADS, HEAD)[:, 1]
        read = jnp.einsum('bmihe,bhef->bmihf', right_q, left, precision=highest)
        scale = weights[CBITS + level_no].reshape(HEADS, blocks, 2, half_size, SPAN)[:, :, 1]
        scale = jnp.transpose(scale, (1, 2, 3, 0)) * (1.0 / math.sqrt(SPAN * half_size * HEAD))
        shaped = inter.reshape(blocks, 2, half_size, SPAN, HEADS, HEAD)
        inter = shaped.at[:, 1].add(read * scale[..., None]).reshape(NCHUNK, SPAN, HEADS, HEAD)
    attended = (intra + inter).reshape(TOKENS, head_cols).astype(jnp.bfloat16)
    return jnp.dot(attended, w_out, preferred_element_type=jnp.float32).astype(jnp.bfloat16)
```

```python
import functools
import math

import jax
import jax.numpy as jnp
from jax import lax
from jax.experimental import pallas as pl
from jax.experimental.pallas import tpu as pltpu
from jax.sharding import PartitionSpec as P

HEADS = 4
HEAD = 256
SPAN = 256
CBITS = 8
TILE = 512
MESH = pl.DeviceIdType.MESH
PIECES = (4, 4, 4)
SHARE = (5, 6, 6)
LAG = (2, 3, 3)
BUDGET = (4, 2, 2)


class Place:
    def __init__(self, groups, seqs):
        self.seqs = seqs
        self.chips = seqs // 2
        self.has_x = groups % 2 == 0
        self.g = lax.axis_index("group")
        self.me = lax.axis_index("seq")
        self.core = lax.rem(self.me, 2)
        self.chip = self.me // 2
        odd = lax.rem(self.chip, 2)
        half = self.chip // 2
        self.pos = half + odd * (self.chips - 1 - 2 * half)
        self.par = lax.rem(self.g, 2)
        self.mate = (self.g, self.me + 1 - 2 * self.core)
        self.cross = (self.g + 1 - 2 * self.par, self.me)

    def chip_at(self, offset):
        pos = lax.rem(self.pos + offset + self.chips, self.chips)
        late = pos // (self.chips // 2)
        return 2 * pos + late * (2 * (self.chips - 1) + 1 - 4 * pos)

    def ring(self, offset):
        return (self.g, self.chip_at(offset) * 2 + self.core)

    def flip(self, bit):
        return (self.g, self.me + (1 - 2 * self.digit(bit)) * 2**bit)

    def digit(self, bit):
        return lax.rem(self.me // 2**bit, 2)

    def greet(self, others):
        barrier = pltpu.get_barrier_semaphore()
        for other in others:
            pl.semaphore_signal(barrier, inc=1, device_id=other, device_id_type=MESH)
        pl.semaphore_wait(barrier, len(others))

    def neighbours(self):
        found = [self.ring(1), self.ring(-1), self.mate]
        return found + [self.cross] if self.has_x else found


class Gather:
    def __init__(self, place, buf, pieces, share, send_sem, recv_sem):
        self.at, self.buf = place, buf
        self.send_sem, self.recv_sem = send_sem, recv_sem
        _, self.rows, self.columns = buf.shape
        self.pieces = max(1, min(pieces, self.rows // 16))
        self.part = self.rows // self.pieces
        self.rel = (self.columns * share // 16) // 128 * 128 if place.has_x else 0
        keep = self.columns - self.rel
        self.ring_cols = (place.par * self.rel, keep) if self.rel else (0, keep)
        self.give_cols = (place.par * keep, self.rel)
        self.take_cols = ((1 - place.par) * keep, self.rel)
        self.every = (0, self.columns)
        self.last = place.chips // 2
        self.slots, self.sent = {}, {}

    def mine(self, offset):
        return self.at.chip_at(offset) * 2 + self.at.core

    def theirs(self, offset):
        return self.at.chip_at(offset) * 2 + 1 - self.at.core

    def span(self, step, d):
        if step < self.last:
            return (0, self.pieces)
        half = self.pieces // 2
        if d == 1:
            return (0, max(half, 1))
        return (half, half)

    def directions(self, step):
        return [d for d in (1, -1) if self.span(step, d)[1]]

    def groups(self, step):
        spans = [(d, self.span(step, d)) for d in self.directions(step)]
        return [[(first + n, d) for d, (first, _) in spans] for n in range(spans[0][1][1])]

    def copy(self, sent, got, index, rows, cols, device):
        start, width = cols
        if not isinstance(start, int):
            start = pl.multiple_of(start, 128)
        first, count = rows
        ref = self.buf.at[index, pl.ds(first * self.part, count * self.part), pl.ds(start, width)]
        return pltpu.make_async_remote_copy(
            src_ref=ref,
            dst_ref=ref,
            send_sem=self.send_sem.at[self.slots.setdefault(("send", *sent), len(self.slots))],
            recv_sem=self.recv_sem.at[self.slots.setdefault(("recv", *got), len(self.slots))],
            device_id=device,
            device_id_type=MESH,
        )

    def send(self, sent, got, index, rows, cols, device):
        self.copy(sent, got, index, rows, cols, device).start()
        before = self.sent.get(sent, (0, cols, device))
        self.sent[sent] = (before[0] + rows[1], cols, device)

    def ring_send(self, step, h, d):
        index = self.mine(-d * (step - 1))
        self.send(("ring", step, d), ("ring", step, d, h), index, (h, 1), self.ring_cols, self.at.ring(d))

    def begin(self):
        for group in zip(*[[(h, d) for h in range(*self.span(1, d))] for d in self.directions(1)]):
            for h, d in group:
                self.ring_send(1, h, d)

    def own(self):
        key = ("mate", 0, 1)
        self.send(key, key, self.at.me, (0, self.pieces), self.every, self.at.mate)

    def arrive(self, step, h, d):
        index = self.mine(-d * step)
        key = ("ring", step, d)
        self.copy(key, (*key, h), index, (h, 1), self.ring_cols, self.at.ring(-d)).wait_recv()
        if step < self.last:
            first, count = self.span(step + 1, d)
            if first <= h < first + count:
                self.ring_send(step + 1, h, d)
        if self.rel:
            key = ("cross", step, d)
            self.send(key, key, index, (h, 1), self.give_cols, self.at.cross)

    def settle(self, step):
        for d in self.directions(step):
            index = self.mine(-d * step)
            rows = self.span(step, d)
            if self.rel:
                key = ("cross", step, d)
                self.copy(key, key, index, rows, self.take_cols, self.at.cross).wait_recv()
            key = ("mate", step, d)
            self.send(key, key, index, rows, self.every, self.at.mate)

    def complete(self, step):
        for d in self.directions(step) if step else (1,):
            key = ("mate", step, d)
            rows = self.span(step, d) if step else (0, self.pieces)
            self.copy(key, key, self.theirs(-d * step), rows, self.every, self.at.mate).wait_recv()

    def offsets(self, step):
        return (step, -step) if 0 < step < self.last else (step,)

    def drain(self, keep=()):
        for sent, (count, cols, device) in list(self.sent.items()):
            if sent[1] not in keep:
                self.copy(sent, sent, 0, (0, count), cols, device).wait_send()
                del self.sent[sent]


def slots_needed(seqs):
    return (seqs // 4) * 20 + 8


class Exchange:
    def __init__(self, place, left, send_sem, recv_sem):
        self.at, self.left = place, left
        self.send_sem, self.recv_sem = send_sem, recv_sem
        self.slots, self.sent = {}, []
        self.c, self.y = place.core, place.digit(1)
        self.head = 2 * self.c + self.y
        self.other = 2 * self.c + 1 - self.y
        self.mate_head = 2 * (1 - self.c) + self.y
        self.mate_other = 2 * (1 - self.c) + 1 - self.y

    def copy(self, key, src, bit, head, device):
        slot = self.slots.setdefault(key, len(self.slots))
        return pltpu.make_async_remote_copy(
            src_ref=src,
            dst_ref=self.left.at[bit, head],
            send_sem=self.send_sem.at[slot],
            recv_sem=self.recv_sem.at[slot],
            device_id=device,
            device_id_type=MESH,
        )

    def send(self, *args):
        one = self.copy(*args)
        one.start()
        self.sent.append(one)

    def forward(self, key, bit, head, device):
        self.send(key, self.left.at[bit, head], bit, head, device)

    def wait(self, key, bit, head, device):
        self.copy(key, self.left.at[bit, head], bit, head, device).wait_recv()

    def spread(self, bit):
        self.forward(("quad", bit), bit, self.head, self.at.flip(1))
        self.forward(("near", bit), bit, self.head, self.at.mate)

    def collect(self, bit):
        if bit > 1:
            self.wait(("quad", bit), bit, self.other, self.at.flip(1))
        else:
            self.wait(("across", 1), bit, self.other, self.at.flip(1))
        self.forward(("far", bit), bit, self.other, self.at.mate)

    def finish(self, bit):
        self.wait(("near", bit), bit, self.mate_head, self.at.mate)
        self.wait(("far", bit), bit, self.mate_other, self.at.mate)

    def drain(self):
        for one in self.sent:
            one.wait_send()


def product(a, b, dims):
    return lax.dot_general(a, b, (dims, ((), ())), preferred_element_type=jnp.float32)


def head_cols(h):
    return pl.ds(h * HEAD, HEAD)


def layer_kernel(
    groups, seqs, tokens_hbm, w_ref, wo_ref, lw_ref, att_hbm, wo_buf,
    tokens_ref, kv_buf, q_buf, total, qkv, mix, acc, attended, flat, weight_ref, local_sum, first_sum, give, pair,
    pair_give, run_give, left, load_sem, kv_send, kv_recv, q_send, q_recv, wo_send, wo_recv, ex_send, ex_recv,
):
    place = Place(groups, seqs)
    rows_w, columns = w_ref.shape
    wide = HEADS * HEAD
    here = place.me
    loads = [
        pltpu.make_async_copy(src, dst, load_sem.at[n])
        for n, (src, dst) in enumerate(
            (
                (w_ref.at[:, pl.ds(wide, columns - wide)], kv_buf.at[here]),
                (w_ref.at[:, pl.ds(0, wide)], q_buf.at[here]),
                (wo_ref, wo_buf.at[here]),
                (tokens_hbm, tokens_ref),
            )
        )
    ]
    for one in loads:
        one.start()
    seq_bits = seqs.bit_length() - 1
    place.greet(place.neighbours() + [place.flip(b) for b in range(1, seq_bits)])
    kv = Gather(place, kv_buf, PIECES[0], SHARE[0], kv_send, kv_recv)
    q = Gather(place, q_buf, PIECES[1], SHARE[1], q_send, q_recv)
    wo = Gather(place, wo_buf, PIECES[2], SHARE[2], wo_send, wo_recv)
    streams = (kv, q, wo)
    last = kv.last
    loads[0].wait()
    kv.begin()
    kv.own()
    for one in loads[1:]:
        one.wait()
    q.own()
    wo.own()

    count = tokens_ref.shape[0] // SPAN
    levels, heads, tokens_here = lw_ref.shape

    for level in range(levels):
        flat[level * heads : (level + 1) * heads, :] = lw_ref[level]
    spare = flat.shape[0] - levels * heads
    if spare:
        flat[levels * heads :, :] = jnp.zeros((spare, tokens_here), jnp.float32)
    weight_ref[...] = flat[...].T

    def mixing(c, h):
        rows = pl.ds(c * SPAN, SPAN)
        i = lax.broadcasted_iota(jnp.int32, (SPAN, SPAN), 0)
        j = lax.broadcasted_iota(jnp.int32, (SPAN, SPAN), 1)
        apart = i ^ j
        value = jnp.zeros((SPAN, SPAN), jnp.float32)
        for level in range(CBITS + 1):
            gain = 1.0 / math.sqrt(HEAD * max(1, 2 ** (level - 1)))
            column = weight_ref[rows, level * HEADS + h : level * HEADS + h + 1] * gain
            column = jnp.broadcast_to(column, (SPAN, SPAN))
            value = column if level == 0 else jnp.where(apart >= 2 ** (level - 1), column, value)
        mix[c, h] = jnp.where(i >= j, value, 0.0)

    aligned = (2 * rows_w) % 128 == 0

    def use(stream, base, step, tile):
        if not aligned:
            return
        cols = pl.ds(tile * TILE, TILE)
        y = None
        for offset in stream.offsets(step):
            chip = place.chip_at(offset)
            x = tokens_ref[:, pl.ds(pl.multiple_of(chip * (2 * rows_w), 128), 2 * rows_w)]
            w = stream.buf[pl.ds(chip * 2, 2), :, cols].reshape(2 * rows_w, TILE)
            part = jnp.dot(x, w, preferred_element_type=jnp.float32)
            y = part if y is None else y + part
        if step:
            y = total[:, pl.ds(base + tile * TILE, TILE)] + y
        if step < last:
            total[:, pl.ds(base + tile * TILE, TILE)] = y
        else:
            qkv[:, pl.ds(base + tile * TILE, TILE)] = y.astype(qkv.dtype)

    def at_once(stream, base):
        if aligned:
            return

        @pl.loop(0, stream.columns // TILE)
        def _(t):
            cols = pl.ds(pl.multiple_of(t * TILE, TILE), TILE)
            w = stream.buf[:, :, cols].reshape(seqs * rows_w, TILE)
            y = jnp.dot(tokens_ref[...], w, preferred_element_type=jnp.float32)
            qkv[:, pl.ds(pl.multiple_of(base + t * TILE, TILE), TILE)] = y.astype(qkv.dtype)

    exchange = Exchange(place, left, ex_send, ex_recv)

    def states(h):
        for c in range(count):
            k = qkv[pl.ds(c * SPAN, SPAN), head_cols(HEADS + h)]
            v = qkv[pl.ds(c * SPAN, SPAN), head_cols(2 * HEADS + h)]
            state = product(k, v, ((0,), (0,)))
            if c == 0:
                local_sum[h] = state
                first_sum[h] = state.astype(jnp.bfloat16)
            else:
                local_sum[h] += state
        give[h] = local_sum[h].astype(jnp.bfloat16)
        exchange.send(("core", h), give.at[h], 0, h, place.mate)

    running = {}

    def exchange_core():
        for h in range(HEADS):
            exchange.wait(("core", h), 0, h, place.mate)
        for n in range(2):
            h = 2 * place.core + n
            pair[n] = local_sum[h] + left[0, h].astype(jnp.float32)
            pair_give[n] = pair[n].astype(jnp.bfloat16)
        y = place.digit(1)
        for n, which in enumerate((1 - y, y)):
            exchange.send(("across", n), pair_give.at[which], 1, 2 * place.core + which, place.flip(1))

    def exchange_across():
        y = place.digit(1)
        exchange.wait(("across", 0), 1, exchange.head, place.flip(1))
        pair[0] = pair[y] + left[1, exchange.head].astype(jnp.float32)
        run_give[2] = pair[0].astype(jnp.bfloat16)
        exchange.send(("hop", 2), run_give.at[2], 2, exchange.head, place.flip(2))
        exchange.forward(("near", 1), 1, exchange.head, place.mate)

    def exchange_hop(bit):
        exchange.wait(("hop", bit), bit, exchange.head, place.flip(bit))
        if bit + 1 < seq_bits:
            pair[0] += left[bit, exchange.head].astype(jnp.float32)
            run_give[bit + 1] = pair[0].astype(jnp.bfloat16)
            exchange.send(("hop", bit + 1), run_give.at[bit + 1], bit + 1, exchange.head, place.flip(bit + 1))
        exchange.spread(bit)

    local_bits = count.bit_length() - 1

    def gain_of(level):
        return 1.0 / math.sqrt(SPAN * 2 ** (level - 1) * HEAD)

    def weight_of(rows, level, h):
        at = (CBITS + level) * HEADS + h
        return weight_ref[rows, at : at + 1]

    def attend(c, h):
        rows = pl.ds(c * SPAN, SPAN)
        qs = qkv[rows, head_cols(h)]
        k = qkv[rows, head_cols(HEADS + h)]
        v = qkv[rows, head_cols(2 * HEADS + h)]
        scores = product(qs, k, ((1,), (1,)))
        probs = (scores * mix[c, h]).astype(jnp.bfloat16)
        got = product(probs, v, ((1,), (0,)))
        if c > 0:
            got += product(qs, first_sum[h], ((1,), (0,))) * (weight_of(rows, 1, h) * gain_of(1))
        acc[rows, head_cols(h)] = got

    def read(bit, h):
        level = local_bits + bit + 1
        scale = place.digit(bit).astype(jnp.float32) * gain_of(level)
        rows = pl.ds(0, count * SPAN)
        got = product(qkv[:, head_cols(h)], left[bit, h], ((1,), (0,)))
        got = acc[:, head_cols(h)] + got * (weight_of(rows, level, h) * scale)
        if bit == seq_bits - 1:
            attended[:, head_cols(h)] = got.astype(jnp.bfloat16)
        else:
            acc[:, head_cols(h)] = got

    store = pltpu.make_async_copy(attended, att_hbm, load_sem.at[0])

    plan, end = [], {}
    for n, stream in enumerate(streams):
        for step in range(1, last + 1):
            for group in stream.groups(step):
                plan.append((n, step, group))
            end[n, step] = len(plan) - 1
    items = []

    def add(ready, cost, fn, *args):
        items.append((ready, cost, functools.partial(fn, *args)))

    for c in range(count):
        for h in range(HEADS):
            add(0, 1, mixing, c, h)
    for n, (stream, base) in enumerate(((kv, wide), (q, 0))):
        for step in range(last + 1):
            ready = end[n, step] + LAG[n] + 1 if step else (0 if n == 0 else end[0, last] + 1)
            add(ready, 0, stream.complete, step)
            for tile in range(stream.columns // TILE):
                add(ready, 2 if stream.offsets(step)[1:] else 1, use, stream, base, step, tile)
        add(0, 0, at_once, stream, base)
        if n == 0:
            ready = end[0, last] + LAG[0] + 1
            for h in range(HEADS):
                add(ready, 1, states, h)
    steps = [exchange_core, exchange_across] + [functools.partial(exchange_hop, b) for b in range(2, seq_bits)]
    ex_items = []
    at = end[0, last] + LAG[0] + 4
    for n, fn in enumerate(steps):
        ex_items.append((at + EX_FIRST + n * EX_LAG, fn))
        if n > 1:
            ex_items.append((at + EX_FIRST + n * EX_LAG + 1, functools.partial(exchange.collect, n - 1)))
    done_q = end[1, last] + LAG[1] + 1
    for c in range(count):
        for h in range(HEADS):
            add(done_q, 1, attend, c, h)

    settles = {}
    for n, stream in enumerate(streams):
        for step in range(1, last + 1):
            settles.setdefault(end[n, step] + LAG[n], []).append(functools.partial(stream.settle, step))

    starts = {}
    for n in (1, 2):
        starts.setdefault(end[n - 1, last - 1 - AHEAD] + 1 if last - 1 - AHEAD > 0 else 0, []).append(streams[n].begin)

    def run(tick, budget):
        for fn in settles.pop(tick, ()):
            fn()
        while ex_items and ex_items[0][0] <= tick and tick < len(plan):
            ready_at, fn = ex_items[0]
            if any(item[2].func is states or item[2].func is use and item[2].args[0] is kv for item in items):
                break
            ex_items.pop(0)
            fn()
        spent = 0
        while items and items[0][0] <= tick and (spent == 0 or spent + items[0][1] <= budget):
            _, cost, fn = items.pop(0)
            fn()
            spent += cost

    for tick, (n, step, group) in enumerate(plan):
        for fn in starts.pop(tick, ()):
            fn()
        for h, d in group:
            streams[n].arrive(step, h, d)
        run(tick, BUDGET[n])
    while items:
        run(10**6, 10**6)
    for _, fn in ex_items:
        fn()
    exchange.collect(seq_bits - 1)
    for tick in sorted(settles):
        for fn in settles[tick]:
            fn()
    for bit in range(seq_bits):
        if bit:
            exchange.finish(bit)
        for h in range(HEADS):
            read(bit, h)
    store.start()
    kv.drain()
    q.drain()
    exchange.drain()
    for step in range(last + 1):
        wo.complete(step)
    wo.drain()
    store.wait()


def project_kernel(x_ref, w_ref, out_ref):
    out_ref[...] = jnp.dot(x_ref[...], w_ref[...], preferred_element_type=jnp.float32).astype(out_ref.dtype)


AHEAD = 0
EX_FIRST = 1
EX_LAG = 4


def on_device(tokens, w_qkv, w_out, level_weight):
    groups, seqs = lax.axis_size("group"), lax.axis_size("seq")
    rows = tokens.shape[0]
    count = rows // SPAN
    seq_bits = seqs.bit_length() - 1
    wide = HEADS * HEAD
    square = (HEAD, HEAD)
    flat_rows = -(-level_weight.shape[0] * level_weight.shape[1] // 8) * 8
    vmem = pl.BlockSpec(memory_space=pltpu.VMEM)
    hbm = pl.BlockSpec(memory_space=pl.ANY)
    sems = pltpu.SemaphoreType.DMA((slots_needed(seqs),))
    attended, wo_full = pl.pallas_call(
        functools.partial(layer_kernel, groups, seqs),
        out_shape=(
            jax.ShapeDtypeStruct((rows, wide), jnp.bfloat16),
            jax.ShapeDtypeStruct((seqs, *w_out.shape), jnp.bfloat16),
        ),
        in_specs=[hbm, hbm, hbm, vmem],
        out_specs=(hbm, hbm),
        scratch_shapes=[
            pltpu.VMEM(tokens.shape, jnp.bfloat16),
            pltpu.VMEM((seqs, w_qkv.shape[0], 2 * wide), jnp.bfloat16),
            pltpu.VMEM((seqs, w_qkv.shape[0], wide), jnp.bfloat16),
            pltpu.VMEM((rows, w_qkv.shape[1]), jnp.float32),
            pltpu.VMEM((rows, w_qkv.shape[1]), jnp.bfloat16),
            pltpu.VMEM((count, HEADS, SPAN, SPAN), jnp.float32),
            pltpu.VMEM((rows, wide), jnp.float32),
            pltpu.VMEM((rows, wide), jnp.bfloat16),
            pltpu.VMEM((flat_rows, rows), jnp.float32),
            pltpu.VMEM((rows, flat_rows), jnp.float32),
            pltpu.VMEM((HEADS, *square), jnp.float32),
            pltpu.VMEM((HEADS, *square), jnp.bfloat16),
            pltpu.VMEM((HEADS, *square), jnp.bfloat16),
            pltpu.VMEM((2, *square), jnp.float32),
            pltpu.VMEM((2, *square), jnp.bfloat16),
            pltpu.VMEM((seq_bits, *square), jnp.bfloat16),
            pltpu.VMEM((seq_bits, HEADS, *square), jnp.bfloat16),
            pltpu.SemaphoreType.DMA((4,)),
            sems, sems, sems, sems, sems, sems,
            pltpu.SemaphoreType.DMA((8 * seq_bits,)),
            pltpu.SemaphoreType.DMA((8 * seq_bits,)),
        ],
        compiler_params=pltpu.CompilerParams(
            collective_id=0, has_side_effects=True, vmem_limit_bytes=58 * 1024 * 1024
        ),
    )(tokens, w_qkv, w_out, level_weight)
    w_whole = wo_full.reshape(seqs * w_out.shape[0], w_out.shape[1])
    return pl.pallas_call(
        project_kernel,
        out_shape=jax.ShapeDtypeStruct((rows, w_out.shape[1]), jnp.bfloat16),
        grid=(w_out.shape[1] // TILE,),
        in_specs=[
            pl.BlockSpec((rows, wide), lambda j: (0, 0)),
            pl.BlockSpec((wide, TILE), lambda j: (0, j)),
        ],
        out_specs=pl.BlockSpec((rows, TILE), lambda j: (0, j)),
        compiler_params=pltpu.CompilerParams(vmem_limit_bytes=24 * 1024 * 1024),
    )(attended, w_whole)


def solution(mesh):
    return jax.shard_map(
        on_device,
        mesh=mesh,
        in_specs=(
            P(("group", "seq"), None),
            P("seq", None),
            P("seq", None),
            P(None, None, ("group", "seq")),
        ),
        out_specs=P(("group", "seq"), None),
        check_vma=False,
    )
```

```python
import functools
import math

import jax
import jax.numpy as jnp
from jax import lax
from jax.experimental import pallas as pl
from jax.experimental.pallas import tpu as pltpu
from jax.sharding import PartitionSpec as P

HEADS = 4
HEAD = 256
SPAN = 256
CBITS = 8
TILE = 512
MESH = pl.DeviceIdType.MESH
PIECES = (4, 4, 4)
SHARE = (5, 6, 6)
LAG = (3, 5, 5)
CLAG = (1, 2, 2)
BUDGET = (4, 2, 2)
EX_FIRST = 3
EX_LAG = 7
APART = 1


class Place:
    def __init__(self, groups, seqs):
        self.seqs = seqs
        self.chips = seqs // 2
        self.has_x = groups % 2 == 0
        self.g = lax.axis_index("group")
        self.me = lax.axis_index("seq")
        self.core = lax.rem(self.me, 2)
        self.chip = self.me // 2
        odd = lax.rem(self.chip, 2)
        half = self.chip // 2
        self.pos = half + odd * (self.chips - 1 - 2 * half)
        self.par = lax.rem(self.g, 2)
        self.mate = (self.g, self.me + 1 - 2 * self.core)
        self.cross = (self.g + 1 - 2 * self.par, self.me)

    def chip_at(self, offset):
        pos = lax.rem(self.pos + offset + self.chips, self.chips)
        late = pos // (self.chips // 2)
        return 2 * pos + late * (2 * (self.chips - 1) + 1 - 4 * pos)

    def ring(self, offset):
        return (self.g, self.chip_at(offset) * 2 + self.core)

    def flip(self, bit):
        return (self.g, self.me + (1 - 2 * self.digit(bit)) * 2**bit)

    def aslant(self, bit):
        return (self.g, self.flip(bit)[1] + (1 - 2 * self.digit(1)) * 2)

    def digit(self, bit):
        return lax.rem(self.me // 2**bit, 2)

    def greet(self, others):
        barrier = pltpu.get_barrier_semaphore()
        for other in others:
            pl.semaphore_signal(barrier, inc=1, device_id=other, device_id_type=MESH)
        pl.semaphore_wait(barrier, len(others))

    def neighbours(self):
        found = [self.ring(1), self.ring(-1), self.mate]
        return found + [self.cross] if self.has_x else found


class Gather:
    def __init__(self, place, buf, pieces, share, send_sem, recv_sem):
        self.at, self.buf = place, buf
        self.send_sem, self.recv_sem = send_sem, recv_sem
        _, self.rows, self.columns = buf.shape
        self.pieces = max(1, min(pieces, self.rows // 16))
        self.part = self.rows // self.pieces
        self.rel = (self.columns * share // 16) // 128 * 128 if place.has_x else 0
        keep = self.columns - self.rel
        self.ring_cols = (place.par * self.rel, keep) if self.rel else (0, keep)
        self.give_cols = (place.par * keep, self.rel)
        self.take_cols = ((1 - place.par) * keep, self.rel)
        self.every = (0, self.columns)
        self.last = place.chips // 2
        self.slots, self.sent = {}, {}
        self.waiting = {}
        for d in self.directions(1):
            first, count = self.span(1, d)
            self.waiting[d] = list(range(first, first + count))

    def mine(self, offset):
        return self.at.chip_at(offset) * 2 + self.at.core

    def theirs(self, offset):
        return self.at.chip_at(offset) * 2 + 1 - self.at.core

    def span(self, step, d):
        if step < self.last:
            return (0, self.pieces)
        half = self.pieces // 2
        if d == 1:
            return (0, max(half, 1))
        return (half, half)

    def directions(self, step):
        return [d for d in (1, -1) if self.span(step, d)[1]]

    def groups(self, step):
        spans = [(d, self.span(step, d)) for d in self.directions(step)]
        return [[(first + n, d) for d, (first, _) in spans] for n in range(spans[0][1][1])]

    def copy(self, sent, got, index, rows, cols, device):
        start, width = cols
        if not isinstance(start, int):
            start = pl.multiple_of(start, 128)
        first, count = rows
        ref = self.buf.at[index, pl.ds(first * self.part, count * self.part), pl.ds(start, width)]
        return pltpu.make_async_remote_copy(
            src_ref=ref,
            dst_ref=ref,
            send_sem=self.send_sem.at[self.slots.setdefault(("send", *sent), len(self.slots))],
            recv_sem=self.recv_sem.at[self.slots.setdefault(("recv", *got), len(self.slots))],
            device_id=device,
            device_id_type=MESH,
        )

    def send(self, sent, got, index, rows, cols, device):
        self.copy(sent, got, index, rows, cols, device).start()
        before = self.sent.get(sent, (0, cols, device))
        self.sent[sent] = (before[0] + rows[1], cols, device)

    def ring_send(self, step, h, d):
        index = self.mine(-d * (step - 1))
        self.send(("ring", step, d), ("ring", step, d, h), index, (h, 1), self.ring_cols, self.at.ring(d))

    def begin(self, d):
        left = self.waiting.get(d)
        if left:
            self.ring_send(1, left.pop(0), d)

    def begin_all(self):
        for _ in range(self.pieces):
            for d in (1, -1):
                self.begin(d)

    def own(self):
        key = ("mate", 0, 1)
        self.send(key, key, self.at.me, (0, self.pieces), self.every, self.at.mate)

    def arrive(self, step, h, d, behind):
        index = self.mine(-d * step)
        key = ("ring", step, d)
        self.copy(key, (*key, h), index, (h, 1), self.ring_cols, self.at.ring(-d)).wait_recv()
        first, count = self.span(step + 1, d) if step < self.last else (0, 0)
        if first <= h < first + count:
            self.ring_send(step + 1, h, d)
        elif behind:
            behind.begin(d)
        if self.rel:
            key = ("cross", step, d)
            self.send(key, key, index, (h, 1), self.give_cols, self.at.cross)

    def settle(self, step):
        for d in self.directions(step):
            index = self.mine(-d * step)
            rows = self.span(step, d)
            if self.rel:
                key = ("cross", step, d)
                self.copy(key, key, index, rows, self.take_cols, self.at.cross).wait_recv()
            key = ("mate", step, d)
            self.send(key, key, index, rows, self.every, self.at.mate)

    def complete(self, step):
        for d in self.directions(step) if step else (1,):
            key = ("mate", step, d)
            rows = self.span(step, d) if step else (0, self.pieces)
            self.copy(key, key, self.theirs(-d * step), rows, self.every, self.at.mate).wait_recv()

    def offsets(self, step):
        return (step, -step) if 0 < step < self.last else (step,)

    def drain(self, keep=()):
        for sent, (count, cols, device) in list(self.sent.items()):
            if sent[1] not in keep:
                self.copy(sent, sent, 0, (0, count), cols, device).wait_send()
                del self.sent[sent]


def slots_needed(seqs):
    return (seqs // 4) * 20 + 8


class Exchange:
    def __init__(self, place, left, bits, send_sem, recv_sem):
        self.at, self.left, self.bits = place, left, bits
        self.send_sem, self.recv_sem = send_sem, recv_sem
        self.slots, self.sent = {}, []
        self.c, self.y = place.core, place.digit(1)
        self.head = 2 * self.c + self.y
        self.other = 2 * self.c + 1 - self.y
        self.mate_head = 2 * (1 - self.c) + self.y
        self.mate_other = 2 * (1 - self.c) + 1 - self.y

    def copy(self, key, src, bit, head, device):
        slot = self.slots.setdefault(key, len(self.slots))
        return pltpu.make_async_remote_copy(
            src_ref=src,
            dst_ref=self.left.at[bit, head],
            send_sem=self.send_sem.at[slot],
            recv_sem=self.recv_sem.at[slot],
            device_id=device,
            device_id_type=MESH,
        )

    def reads(self, bit):
        return self.at.digit(bit) == 1

    def end(self):
        return self.at.me // 4 == self.at.seqs // 4 - 1

    def send(self, when, *args):
        self.sent.append((when, args))
        guarded(when, lambda: self.copy(*args).start())

    def forward(self, when, key, bit, head, device):
        self.send(when, key, self.left.at[bit, head], bit, head, device)

    def wait(self, when, key, bit, head, device):
        guarded(when, lambda: self.copy(key, self.left.at[bit, head], bit, head, device).wait_recv())

    def hop(self, bit, src):
        top = bit == self.bits - 1
        self.send(self.at.digit(bit) == 0 if top else None, ("hop", bit), src, bit, self.head, self.at.flip(bit))
        if top:
            near_end = self.at.me // 4 == self.at.seqs // 4 - 1 - 2**bit // 4
            self.send(near_end, ("diag", bit), src, bit, self.head, self.at.aslant(bit))

    def hopped(self, bit):
        top = bit == self.bits - 1
        self.wait(self.reads(bit) if top else None, ("hop", bit), bit, self.head, self.at.flip(bit))

    def spread(self, bit):
        reads = self.reads(bit)
        if bit > 1:
            quad = jnp.logical_and(reads, jnp.logical_not(self.end())) if bit == self.bits - 1 else reads
            self.forward(quad, ("quad", bit), bit, self.head, self.at.flip(1))
        self.forward(reads, ("near", bit), bit, self.head, self.at.mate)

    def collect(self, bit):
        reads = self.reads(bit)
        if bit == 1:
            self.wait(reads, ("across", 1), bit, self.other, self.at.flip(1))
        elif bit == self.bits - 1:
            quad = jnp.logical_and(reads, jnp.logical_not(self.end()))
            self.wait(quad, ("quad", bit), bit, self.other, self.at.flip(1))
            self.wait(self.end(), ("diag", bit), bit, self.other, self.at.aslant(bit))
        else:
            self.wait(reads, ("quad", bit), bit, self.other, self.at.flip(1))
        self.forward(reads, ("far", bit), bit, self.other, self.at.mate)

    def finish(self, bit):
        self.wait(self.reads(bit), ("near", bit), bit, self.mate_head, self.at.mate)
        self.wait(self.reads(bit), ("far", bit), bit, self.mate_other, self.at.mate)

    def drain(self):
        for when, args in self.sent:
            guarded(when, lambda: self.copy(*args).wait_send())


def guarded(when, fn):
    if when is None:
        fn()
    else:
        pl.when(when)(fn)


def product(a, b, dims):
    return lax.dot_general(a, b, (dims, ((), ())), preferred_element_type=jnp.float32)


def head_cols(h):
    return pl.ds(h * HEAD, HEAD)


def layer_kernel(
    groups, seqs, tokens_hbm, w_ref, wo_ref, lw_hbm, out_ref,
    tokens_ref, kv_buf, q_buf, wo_buf, total, qkv, mix, acc, attended, lw_ref, flat, weight_ref, local_sum, first_sum, give, pair,
    pair_give, run_give, left, load_sem, kv_send, kv_recv, q_send, q_recv, wo_send, wo_recv, ex_send, ex_recv,
):
    place = Place(groups, seqs)
    rows_w, columns = w_ref.shape
    wide = HEADS * HEAD
    here = place.me
    loads = [
        pltpu.make_async_copy(src, dst, load_sem.at[n])
        for n, (src, dst) in enumerate(
            (
                (w_ref.at[:, pl.ds(wide, columns - wide)], kv_buf.at[here]),
                (w_ref.at[:, pl.ds(0, wide)], q_buf.at[here]),
                (wo_ref, wo_buf.at[here]),
                (lw_hbm, lw_ref),
                (tokens_hbm, tokens_ref),
            )
        )
    ]
    for one in loads:
        one.start()
    seq_bits = seqs.bit_length() - 1
    place.greet(place.neighbours() + [place.flip(b) for b in range(1, seq_bits)] + [place.aslant(seq_bits - 1)])
    kv = Gather(place, kv_buf, PIECES[0], SHARE[0], kv_send, kv_recv)
    q = Gather(place, q_buf, PIECES[1], SHARE[1], q_send, q_recv)
    wo = Gather(place, wo_buf, PIECES[2], SHARE[2], wo_send, wo_recv)
    streams = (kv, q, wo)
    last = kv.last
    loads[0].wait()
    kv.begin_all()
    kv.own()
    for one in loads[1:]:
        one.wait()
    for stream in streams[1:]:
        stream.own()

    count = tokens_ref.shape[0] // SPAN
    levels, heads, tokens_here = lw_ref.shape

    for level in range(levels):
        flat[level * heads : (level + 1) * heads, :] = lw_ref[level]
    spare = flat.shape[0] - levels * heads
    if spare:
        flat[levels * heads :, :] = jnp.zeros((spare, tokens_here), jnp.float32)
    weight_ref[...] = flat[...].T

    def mixing(c, h):
        rows = pl.ds(c * SPAN, SPAN)
        i = lax.broadcasted_iota(jnp.int32, (SPAN, SPAN), 0)
        j = lax.broadcasted_iota(jnp.int32, (SPAN, SPAN), 1)
        apart = i ^ j
        value = jnp.zeros((SPAN, SPAN), jnp.float32)
        for level in range(CBITS + 1):
            gain = 1.0 / math.sqrt(HEAD * max(1, 2 ** (level - 1)))
            column = weight_ref[rows, level * HEADS + h : level * HEADS + h + 1] * gain
            column = jnp.broadcast_to(column, (SPAN, SPAN))
            value = column if level == 0 else jnp.where(apart >= 2 ** (level - 1), column, value)
        mix[c, h] = jnp.where(i >= j, value, 0.0)

    aligned = (2 * rows_w) % 128 == 0

    def use(stream, base, step, tile):
        if not aligned:
            return
        cols = pl.ds(tile * TILE, TILE)
        y = None
        for offset in stream.offsets(step):
            chip = place.chip_at(offset)
            x = tokens_ref[:, pl.ds(pl.multiple_of(chip * (2 * rows_w), 128), 2 * rows_w)]
            w = stream.buf[pl.ds(chip * 2, 2), :, cols].reshape(2 * rows_w, TILE)
            part = jnp.dot(x, w, preferred_element_type=jnp.float32)
            y = part if y is None else y + part
        if step:
            y = total[:, pl.ds(base + tile * TILE, TILE)] + y
        if step < last:
            total[:, pl.ds(base + tile * TILE, TILE)] = y
        else:
            qkv[:, pl.ds(base + tile * TILE, TILE)] = y.astype(qkv.dtype)

    def at_once(stream, base):
        if aligned:
            return

        @pl.loop(0, stream.columns // TILE)
        def _(t):
            cols = pl.ds(pl.multiple_of(t * TILE, TILE), TILE)
            w = stream.buf[:, :, cols].reshape(seqs * rows_w, TILE)
            y = jnp.dot(tokens_ref[...], w, preferred_element_type=jnp.float32)
            qkv[:, pl.ds(pl.multiple_of(base + t * TILE, TILE), TILE)] = y.astype(qkv.dtype)

    exchange = Exchange(place, left, seq_bits, ex_send, ex_recv)

    def states(h):
        for c in range(count):
            k = qkv[pl.ds(c * SPAN, SPAN), head_cols(HEADS + h)]
            v = qkv[pl.ds(c * SPAN, SPAN), head_cols(2 * HEADS + h)]
            state = product(k, v, ((0,), (0,)))
            if c == 0:
                local_sum[h] = state
                first_sum[h] = state.astype(jnp.bfloat16)
            else:
                local_sum[h] += state
        give[h] = local_sum[h].astype(jnp.bfloat16)
        exchange.send(None, ("core", h), give.at[h], 0, h, place.mate)

    running = {}

    def exchange_core():
        for h in range(HEADS):
            exchange.wait(None, ("core", h), 0, h, place.mate)
        for n in range(2):
            h = 2 * place.core + n
            pair[n] = local_sum[h] + left[0, h].astype(jnp.float32)
            pair_give[n] = pair[n].astype(jnp.bfloat16)
        y = place.digit(1)
        for n, which in enumerate((1 - y, y)):
            exchange.send(y == 0 if n else None, ("across", n), pair_give.at[which], 1, 2 * place.core + which, place.flip(1))

    def exchange_across():
        y = place.digit(1)
        exchange.wait(None, ("across", 0), 1, exchange.head, place.flip(1))
        pair[0] = pair[y] + left[1, exchange.head].astype(jnp.float32)
        run_give[2] = pair[0].astype(jnp.bfloat16)
        exchange.hop(2, run_give.at[2])
        exchange.spread(1)

    def exchange_hop(bit):
        exchange.hopped(bit)
        if bit + 1 < seq_bits:
            pair[0] += left[bit, exchange.head].astype(jnp.float32)
            run_give[bit + 1] = pair[0].astype(jnp.bfloat16)
            exchange.hop(bit + 1, run_give.at[bit + 1])
        exchange.spread(bit)

    local_bits = count.bit_length() - 1

    def gain_of(level):
        return 1.0 / math.sqrt(SPAN * 2 ** (level - 1) * HEAD)

    def weight_of(rows, level, h):
        at = (CBITS + level) * HEADS + h
        return weight_ref[rows, at : at + 1]

    def attend(c, h):
        rows = pl.ds(c * SPAN, SPAN)
        qs = qkv[rows, head_cols(h)]
        k = qkv[rows, head_cols(HEADS + h)]
        v = qkv[rows, head_cols(2 * HEADS + h)]
        scores = product(qs, k, ((1,), (1,)))
        probs = (scores * mix[c, h]).astype(jnp.bfloat16)
        got = product(probs, v, ((1,), (0,)))
        if c > 0:
            got += product(qs, first_sum[h], ((1,), (0,))) * (weight_of(rows, 1, h) * gain_of(1))
        acc[rows, head_cols(h)] = got

    def read(bit, h):
        level = local_bits + bit + 1
        rows = pl.ds(0, count * SPAN)

        def _():
            got = product(qkv[:, head_cols(h)], left[bit, h], ((1,), (0,)))
            acc[:, head_cols(h)] += got * (weight_of(rows, level, h) * gain_of(level))

        guarded(place.digit(bit) == 1, _)

    def finish():
        attended[...] = acc[...].astype(jnp.bfloat16)

    def project(tile):
        cols = pl.ds(tile * TILE, TILE)
        w = wo_buf[:, :, cols].reshape(wide, TILE)
        out_ref[:, cols] = jnp.dot(attended[...], w, preferred_element_type=jnp.float32).astype(out_ref.dtype)

    order = [(0, step) for step in range(1, last + 1)]
    split = max(last - APART, 0)
    order += [(n, step) for step in range(1, split + 1) for n in (1, 2)]
    order += [(n, step) for n in (1, 2) for step in range(split + 1, last + 1)]
    plan, end = [], {}
    for n, step in order:
        plan += [(n, step, group) for group in streams[n].groups(step)]
        end[n, step] = len(plan) - 1
    items = []

    def add(ready, cost, fn, *args):
        items.append((ready, cost, functools.partial(fn, *args)))

    for c in range(count):
        for h in range(HEADS):
            add(0, 1, mixing, c, h)
    done = {}
    for n, stream in enumerate(streams):
        for step in range(last + 1):
            done[n, step] = end[n, step] + LAG[n] + CLAG[n] if step else (end[0, last] + 1 if n else 0)
    ex_items = []

    def flush():
        while ex_items:
            ex_items.pop(0)[1]()

    for n, base in ((0, wide), (1, 0)):
        for step in range(last + 1):
            add(done[n, step], 0, streams[n].complete, step)
            for tile in range(streams[n].columns // TILE):
                add(done[n, step], 2 if streams[n].offsets(step)[1:] else 1, use, streams[n], base, step, tile)
        add(done[n, last], 0, at_once, streams[n], base)
        for h in range(HEADS) if n == 0 else ():
            add(done[n, last], 1, states, h)
    for h in range(HEADS):
        for c in range(count):
            add(done[1, last], 1, attend, c, h)
    for step in range(last + 1):
        add(done[2, step], 0, wo.complete, step)
    items.sort(key=lambda item: item[0])

    steps = [exchange_core, exchange_across] + [functools.partial(exchange_hop, b) for b in range(2, seq_bits)]
    at = done[0, last] + EX_FIRST
    for n, fn in enumerate(steps):
        ex_items.append((at + n * EX_LAG, fn))
        if n > 1:
            ex_items.append((at + n * EX_LAG + 1, functools.partial(exchange.collect, n - 1)))
    ex_items.append((at + (len(steps) - 1) * EX_LAG + 3, functools.partial(exchange.collect, seq_bits - 1)))
    for bit in range(1, seq_bits):
        ex_items.append((at + (len(steps) - 1) * EX_LAG + 5, functools.partial(exchange.finish, bit)))

    settles = {}
    for n, stream in enumerate(streams):
        for step in range(1, last + 1):
            settles.setdefault(end[n, step] + LAG[n], []).append(functools.partial(stream.settle, step))

    def run(tick, budget):
        for fn in settles.pop(tick, ()):
            fn()
        while ex_items and ex_items[0][0] <= tick and tick < len(plan):
            ready_at, fn = ex_items[0]
            if any(item[2].func is states or item[2].func is use and item[2].args[0] is kv for item in items):
                break
            ex_items.pop(0)
            fn()
        spent = 0
        while items and items[0][0] <= tick and (spent == 0 or spent + items[0][1] <= budget):
            _, cost, fn = items.pop(0)
            fn()
            spent += cost

    for tick, (n, step, group) in enumerate(plan):
        behind = (None if split else wo) if n else q
        for h, d in group:
            streams[n].arrive(step, h, d, behind)
        if tick == end[0, last]:
            q.begin_all()
            if split:
                wo.begin_all()
        if tick == end[1, last]:
            wo.begin_all()
        run(tick, BUDGET[n])
    late = sorted(settles)
    for tick in late[:-1]:
        for fn in settles[tick]:
            fn()
    tail = [fn for _, _, fn in items]
    for fn in tail:
        if fn.func == wo.complete:
            continue
        fn()
    for fn in settles[late[-1]] if late else ():
        fn()
    flush()
    for bit in range(seq_bits):
        for h in range(HEADS):
            read(bit, h)
    finish()
    for fn in tail:
        if fn.func == wo.complete:
            fn()
    for tile in range(wo.columns // TILE):
        project(tile)
    for one in (*streams, exchange):
        one.drain()


def on_device(tokens, w_qkv, w_out, level_weight):
    groups, seqs = lax.axis_size("group"), lax.axis_size("seq")
    rows = tokens.shape[0]
    count = rows // SPAN
    seq_bits = seqs.bit_length() - 1
    wide = HEADS * HEAD
    square = (HEAD, HEAD)
    flat_rows = -(-level_weight.shape[0] * level_weight.shape[1] // 8) * 8
    vmem = pl.BlockSpec(memory_space=pltpu.VMEM)
    hbm = pl.BlockSpec(memory_space=pl.ANY)
    sems = pltpu.SemaphoreType.DMA((slots_needed(seqs),))
    return pl.pallas_call(
        functools.partial(layer_kernel, groups, seqs),
        out_shape=pltpu.VMEM((rows, w_out.shape[1]), jnp.bfloat16),
        in_specs=[hbm, hbm, hbm, hbm],
        out_specs=vmem,
        scratch_shapes=[
            pltpu.VMEM(tokens.shape, jnp.bfloat16),
            pltpu.VMEM((seqs, w_qkv.shape[0], 2 * wide), jnp.bfloat16),
            pltpu.VMEM((seqs, w_qkv.shape[0], wide), jnp.bfloat16),
            pltpu.VMEM((seqs, *w_out.shape), jnp.bfloat16),
            pltpu.VMEM((rows, w_qkv.shape[1]), jnp.float32),
            pltpu.VMEM((rows, w_qkv.shape[1]), jnp.bfloat16),
            pltpu.VMEM((count, HEADS, SPAN, SPAN), jnp.float32),
            pltpu.VMEM((rows, wide), jnp.float32),
            pltpu.VMEM((rows, wide), jnp.bfloat16),
            pltpu.VMEM(level_weight.shape, jnp.float32),
            pltpu.VMEM((flat_rows, rows), jnp.float32),
            pltpu.VMEM((rows, flat_rows), jnp.float32),
            pltpu.VMEM((HEADS, *square), jnp.float32),
            pltpu.VMEM((HEADS, *square), jnp.bfloat16),
            pltpu.VMEM((HEADS, *square), jnp.bfloat16),
            pltpu.VMEM((2, *square), jnp.float32),
            pltpu.VMEM((2, *square), jnp.bfloat16),
            pltpu.VMEM((seq_bits, *square), jnp.bfloat16),
            pltpu.VMEM((seq_bits, HEADS, *square), jnp.bfloat16),
            pltpu.SemaphoreType.DMA((5,)),
            *[sems] * 6,
            pltpu.SemaphoreType.DMA((8 * seq_bits,)),
            pltpu.SemaphoreType.DMA((8 * seq_bits,)),
        ],
        compiler_params=pltpu.CompilerParams(
            collective_id=0, has_side_effects=True, vmem_limit_bytes=58 * 1024 * 1024
        ),
    )(tokens, w_qkv, w_out, level_weight)


def solution(mesh):
    return jax.shard_map(
        on_device,
        mesh=mesh,
        in_specs=(
            P(("group", "seq"), None),
            P("seq", None),
            P("seq", None),
            P(None, None, ("group", "seq")),
        ),
        out_specs=P(("group", "seq"), None),
        check_vma=False,
    )
```

```python
import functools
import math

import jax
import jax.numpy as jnp
from jax import lax
from jax.experimental import pallas as pl
from jax.experimental.pallas import tpu as pltpu
from jax.sharding import PartitionSpec as P

HEADS = 4
HEAD = 256
SPAN = 256
CBITS = 8
TILE = 512
MESH = pl.DeviceIdType.MESH
PIECES = (4, 4, 4)
SHARE = ((5, 6, 6, 6), (4, 6, 6, 6), (5, 6, 6, 6))
LAG = (2, 5, 5)
CLAG = (1, 2, 2)
BUDGET = (4, 2, 2)
EX_FIRST = 4
EX_LAG = 6
APART = 1
BEFORE = 8


class Place:
    def __init__(self, groups, seqs):
        self.seqs = seqs
        self.chips = seqs // 2
        self.has_x = groups % 2 == 0
        self.g = lax.axis_index("group")
        self.me = lax.axis_index("seq")
        self.core = lax.rem(self.me, 2)
        self.chip = self.me // 2
        odd = lax.rem(self.chip, 2)
        half = self.chip // 2
        self.pos = half + odd * (self.chips - 1 - 2 * half)
        self.par = lax.rem(self.g, 2)
        self.mate = (self.g, self.me + 1 - 2 * self.core)
        self.cross = (self.g + 1 - 2 * self.par, self.me)

    def chip_at(self, offset):
        pos = lax.rem(self.pos + offset + self.chips, self.chips)
        late = pos // (self.chips // 2)
        return 2 * pos + late * (2 * (self.chips - 1) + 1 - 4 * pos)

    def ring(self, offset):
        return (self.g, self.chip_at(offset) * 2 + self.core)

    def flip(self, bit):
        return (self.g, self.me + (1 - 2 * self.digit(bit)) * 2**bit)

    def aslant(self, bit):
        return (self.g, self.flip(bit)[1] + (1 - 2 * self.digit(1)) * 2)

    def digit(self, bit):
        return lax.rem(self.me // 2**bit, 2)

    def greet(self, others):
        barrier = pltpu.get_barrier_semaphore()
        for other in others:
            pl.semaphore_signal(barrier, inc=1, device_id=other, device_id_type=MESH)
        pl.semaphore_wait(barrier, len(others))

    def neighbours(self):
        found = [self.ring(1), self.ring(-1), self.mate]
        return found + [self.cross] if self.has_x else found


class Gather:
    def __init__(self, place, buf, pieces, share, send_sem, recv_sem):
        self.at, self.buf = place, buf
        self.send_sem, self.recv_sem = send_sem, recv_sem
        _, self.rows, self.columns = buf.shape
        self.pieces = max(1, min(pieces, self.rows // 16))
        self.part = self.rows // self.pieces
        self.share = share
        self.every = (0, self.columns)
        self.last = place.chips // 2
        self.slots, self.sent = {}, {}
        self.waiting = {}
        for d in self.directions(1):
            self.waiting[d] = self.turn(1, d)

    def rel(self, step):
        share = self.share[(step - 1) * len(self.share) // self.last]
        return (self.columns * share // 16) // 128 * 128 if self.at.has_x else 0

    def ring_cols(self, step):
        rel = self.rel(step)
        return (self.at.par * rel if rel else 0, self.columns - rel)

    def give_cols(self, step):
        return (self.at.par * (self.columns - self.rel(step)), self.rel(step))

    def take_cols(self, step):
        return ((1 - self.at.par) * (self.columns - self.rel(step)), self.rel(step))

    def mine(self, offset):
        return self.at.chip_at(offset) * 2 + self.at.core

    def theirs(self, offset):
        return self.at.chip_at(offset) * 2 + 1 - self.at.core

    def span(self, step, d):
        if step < self.last:
            return (0, self.pieces)
        half = self.pieces // 2
        if d == 1:
            return (0, max(half, 1))
        return (half, half)

    def directions(self, step):
        return [d for d in (1, -1) if self.span(step, d)[1]]

    def turn(self, step, d):
        first, count = self.span(step, d)
        start = self.span(self.last, d)[0] - first
        return [first + (start + n) % count for n in range(count)]

    def groups(self, step):
        turns = [[(h, d) for h in self.turn(step, d)] for d in self.directions(step)]
        return list(zip(*turns))

    def copy(self, sent, got, index, rows, cols, device):
        start, width = cols
        if not isinstance(start, int):
            start = pl.multiple_of(start, 128)
        first, count = rows
        ref = self.buf.at[index, pl.ds(first * self.part, count * self.part), pl.ds(start, width)]
        return pltpu.make_async_remote_copy(
            src_ref=ref,
            dst_ref=ref,
            send_sem=self.send_sem.at[self.slots.setdefault(("send", *sent), len(self.slots))],
            recv_sem=self.recv_sem.at[self.slots.setdefault(("recv", *got), len(self.slots))],
            device_id=device,
            device_id_type=MESH,
        )

    def send(self, sent, got, index, rows, cols, device):
        self.copy(sent, got, index, rows, cols, device).start()
        before = self.sent.get(sent, (0, cols, device))
        self.sent[sent] = (before[0] + rows[1], cols, device)

    def ring_send(self, step, h, d):
        index = self.mine(-d * (step - 1))
        self.send(("ring", step, d), ("ring", step, d, h), index, (h, 1), self.ring_cols(step), self.at.ring(d))

    def begin(self, d):
        left = self.waiting.get(d)
        if left:
            self.ring_send(1, left.pop(0), d)

    def begin_all(self):
        for _ in range(self.pieces):
            for d in (1, -1):
                self.begin(d)

    def own(self):
        key = ("mate", 0, 1)
        self.send(key, key, self.at.me, (0, self.pieces), self.every, self.at.mate)

    def arrive(self, step, h, d, behind):
        index = self.mine(-d * step)
        key = ("ring", step, d)
        self.copy(key, (*key, h), index, (h, 1), self.ring_cols(step), self.at.ring(-d)).wait_recv()
        first, count = self.span(step + 1, d) if step < self.last else (0, 0)
        if first <= h < first + count:
            self.ring_send(step + 1, h, d)
        elif behind:
            behind.begin(d)
        if self.rel(step):
            key = ("cross", step, d)
            self.send(key, key, index, (h, 1), self.give_cols(step), self.at.cross)

    def settle(self, step):
        for d in self.directions(step):
            index = self.mine(-d * step)
            rows = self.span(step, d)
            if self.rel(step):
                key = ("cross", step, d)
                self.copy(key, key, index, rows, self.take_cols(step), self.at.cross).wait_recv()
            key = ("mate", step, d)
            self.send(key, key, index, rows, self.every, self.at.mate)

    def complete(self, step):
        for d in self.directions(step) if step else (1,):
            key = ("mate", step, d)
            rows = self.span(step, d) if step else (0, self.pieces)
            self.copy(key, key, self.theirs(-d * step), rows, self.every, self.at.mate).wait_recv()

    def offsets(self, step):
        return (step, -step) if 0 < step < self.last else (step,)

    def drain(self, keep=()):
        for sent, (count, cols, device) in list(self.sent.items()):
            if sent[1] not in keep:
                self.copy(sent, sent, 0, (0, count), cols, device).wait_send()
                del self.sent[sent]


def slots_needed(seqs):
    return (seqs // 4) * 20 + 8


class Exchange:
    def __init__(self, place, left, bits, send_sem, recv_sem):
        self.at, self.left, self.bits = place, left, bits
        self.send_sem, self.recv_sem = send_sem, recv_sem
        self.slots, self.sent = {}, []
        self.c, self.y = place.core, place.digit(1)
        self.head = 2 * self.c + self.y
        self.other = 2 * self.c + 1 - self.y
        self.mate_head = 2 * (1 - self.c) + self.y
        self.mate_other = 2 * (1 - self.c) + 1 - self.y

    def copy(self, key, src, bit, head, device):
        slot = self.slots.setdefault(key, len(self.slots))
        return pltpu.make_async_remote_copy(
            src_ref=src,
            dst_ref=self.left.at[bit, head],
            send_sem=self.send_sem.at[slot],
            recv_sem=self.recv_sem.at[slot],
            device_id=device,
            device_id_type=MESH,
        )

    def reads(self, bit):
        return self.at.digit(bit) == 1

    def end(self):
        return self.at.me // 4 == self.at.seqs // 4 - 1

    def send(self, when, *args):
        self.sent.append((when, args))
        guarded(when, lambda: self.copy(*args).start())

    def forward(self, when, key, bit, head, device):
        self.send(when, key, self.left.at[bit, head], bit, head, device)

    def wait(self, when, key, bit, head, device):
        guarded(when, lambda: self.copy(key, self.left.at[bit, head], bit, head, device).wait_recv())

    def hop(self, bit, src):
        top = bit == self.bits - 1
        self.send(self.at.digit(bit) == 0 if top else None, ("hop", bit), src, bit, self.head, self.at.flip(bit))
        if top:
            near_end = self.at.me // 4 == self.at.seqs // 4 - 1 - 2**bit // 4
            self.send(near_end, ("diag", bit), src, bit, self.head, self.at.aslant(bit))

    def hopped(self, bit):
        top = bit == self.bits - 1
        self.wait(self.reads(bit) if top else None, ("hop", bit), bit, self.head, self.at.flip(bit))

    def spread(self, bit):
        reads = self.reads(bit)
        if bit > 1:
            quad = jnp.logical_and(reads, jnp.logical_not(self.end())) if bit == self.bits - 1 else reads
            self.forward(quad, ("quad", bit), bit, self.head, self.at.flip(1))
        self.forward(reads, ("near", bit), bit, self.head, self.at.mate)

    def collect(self, bit):
        reads = self.reads(bit)
        if bit == 1:
            self.wait(reads, ("across", 1), bit, self.other, self.at.flip(1))
        elif bit == self.bits - 1:
            quad = jnp.logical_and(reads, jnp.logical_not(self.end()))
            self.wait(quad, ("quad", bit), bit, self.other, self.at.flip(1))
            self.wait(self.end(), ("diag", bit), bit, self.other, self.at.aslant(bit))
        else:
            self.wait(reads, ("quad", bit), bit, self.other, self.at.flip(1))
        self.forward(reads, ("far", bit), bit, self.other, self.at.mate)

    def finish(self, bit):
        self.wait(self.reads(bit), ("near", bit), bit, self.mate_head, self.at.mate)
        self.wait(self.reads(bit), ("far", bit), bit, self.mate_other, self.at.mate)

    def drain(self):
        for when, args in self.sent:
            guarded(when, lambda: self.copy(*args).wait_send())


def guarded(when, fn):
    if when is None:
        fn()
    else:
        pl.when(when)(fn)


def product(a, b, dims):
    return lax.dot_general(a, b, (dims, ((), ())), preferred_element_type=jnp.float32)


def head_cols(h):
    return pl.ds(h * HEAD, HEAD)


def layer_kernel(
    groups, seqs, tokens_hbm, w_ref, wo_ref, lw_hbm, out_ref,
    tokens_ref, kv_buf, q_buf, wo_buf, total, qkv, mix, acc, attended, lw_ref, flat, weight_ref, local_sum, first_sum, give, pair,
    pair_give, run_give, left, load_sem, kv_send, kv_recv, q_send, q_recv, wo_send, wo_recv, ex_send, ex_recv,
):
    place = Place(groups, seqs)
    rows_w, columns = w_ref.shape
    wide = HEADS * HEAD
    here = place.me
    loads = [
        pltpu.make_async_copy(src, dst, load_sem.at[n])
        for n, (src, dst) in enumerate(
            (
                (w_ref.at[:, pl.ds(wide, columns - wide)], kv_buf.at[here]),
                (w_ref.at[:, pl.ds(0, wide)], q_buf.at[here]),
                (wo_ref, wo_buf.at[here]),
                (lw_hbm, lw_ref),
                (tokens_hbm, tokens_ref),
            )
        )
    ]
    for one in loads:
        one.start()
    seq_bits = seqs.bit_length() - 1
    place.greet(place.neighbours() + [place.flip(b) for b in range(1, seq_bits)] + [place.aslant(seq_bits - 1)])
    kv = Gather(place, kv_buf, PIECES[0], SHARE[0], kv_send, kv_recv)
    q = Gather(place, q_buf, PIECES[1], SHARE[1], q_send, q_recv)
    wo = Gather(place, wo_buf, PIECES[2], SHARE[2], wo_send, wo_recv)
    streams = (kv, q, wo)
    last = kv.last
    loads[0].wait()
    kv.begin_all()
    kv.own()
    for one in loads[1:]:
        one.wait()
    for stream in streams[1:]:
        stream.own()

    count = tokens_ref.shape[0] // SPAN
    levels, heads, tokens_here = lw_ref.shape

    for level in range(levels):
        flat[level * heads : (level + 1) * heads, :] = lw_ref[level]
    spare = flat.shape[0] - levels * heads
    if spare:
        flat[levels * heads :, :] = jnp.zeros((spare, tokens_here), jnp.float32)
    weight_ref[...] = flat[...].T

    def mixing(c, h):
        rows = pl.ds(c * SPAN, SPAN)
        i = lax.broadcasted_iota(jnp.int32, (SPAN, SPAN), 0)
        j = lax.broadcasted_iota(jnp.int32, (SPAN, SPAN), 1)
        apart = i ^ j
        value = jnp.zeros((SPAN, SPAN), jnp.float32)
        for level in range(CBITS + 1):
            gain = 1.0 / math.sqrt(HEAD * max(1, 2 ** (level - 1)))
            column = weight_ref[rows, level * HEADS + h : level * HEADS + h + 1] * gain
            column = jnp.broadcast_to(column, (SPAN, SPAN))
            value = column if level == 0 else jnp.where(apart >= 2 ** (level - 1), column, value)
        mix[c, h] = jnp.where(i >= j, value, 0.0)

    aligned = (2 * rows_w) % 128 == 0

    def use(stream, base, step, tile):
        if not aligned:
            return
        cols = pl.ds(tile * TILE, TILE)
        y = None
        for offset in stream.offsets(step):
            chip = place.chip_at(offset)
            x = tokens_ref[:, pl.ds(pl.multiple_of(chip * (2 * rows_w), 128), 2 * rows_w)]
            w = stream.buf[pl.ds(chip * 2, 2), :, cols].reshape(2 * rows_w, TILE)
            part = jnp.dot(x, w, preferred_element_type=jnp.float32)
            y = part if y is None else y + part
        if step:
            y = total[:, pl.ds(base + tile * TILE, TILE)] + y
        if step < last:
            total[:, pl.ds(base + tile * TILE, TILE)] = y
        else:
            qkv[:, pl.ds(base + tile * TILE, TILE)] = y.astype(qkv.dtype)

    def at_once(stream, base):
        if aligned:
            return

        @pl.loop(0, stream.columns // TILE)
        def _(t):
            cols = pl.ds(pl.multiple_of(t * TILE, TILE), TILE)
            w = stream.buf[:, :, cols].reshape(seqs * rows_w, TILE)
            y = jnp.dot(tokens_ref[...], w, preferred_element_type=jnp.float32)
            qkv[:, pl.ds(pl.multiple_of(base + t * TILE, TILE), TILE)] = y.astype(qkv.dtype)

    exchange = Exchange(place, left, seq_bits, ex_send, ex_recv)

    def states(h):
        for c in range(count):
            k = qkv[pl.ds(c * SPAN, SPAN), head_cols(HEADS + h)]
            v = qkv[pl.ds(c * SPAN, SPAN), head_cols(2 * HEADS + h)]
            state = product(k, v, ((0,), (0,)))
            if c == 0:
                local_sum[h] = state
                first_sum[h] = state.astype(jnp.bfloat16)
            else:
                local_sum[h] += state
        give[h] = local_sum[h].astype(jnp.bfloat16)
        exchange.send(None, ("core", h), give.at[h], 0, h, place.mate)

    running = {}

    def exchange_core():
        for h in range(HEADS):
            exchange.wait(None, ("core", h), 0, h, place.mate)
        for n in range(2):
            h = 2 * place.core + n
            pair[n] = local_sum[h] + left[0, h].astype(jnp.float32)
            pair_give[n] = pair[n].astype(jnp.bfloat16)
        y = place.digit(1)
        for n, which in enumerate((1 - y, y)):
            exchange.send(y == 0 if n else None, ("across", n), pair_give.at[which], 1, 2 * place.core + which, place.flip(1))

    def exchange_across():
        y = place.digit(1)
        exchange.wait(None, ("across", 0), 1, exchange.head, place.flip(1))
        pair[0] = pair[y] + left[1, exchange.head].astype(jnp.float32)
        run_give[2] = pair[0].astype(jnp.bfloat16)
        exchange.hop(2, run_give.at[2])
        exchange.spread(1)

    def exchange_hop(bit):
        exchange.hopped(bit)
        if bit + 1 < seq_bits:
            pair[0] += left[bit, exchange.head].astype(jnp.float32)
            run_give[bit + 1] = pair[0].astype(jnp.bfloat16)
            exchange.hop(bit + 1, run_give.at[bit + 1])
        exchange.spread(bit)

    local_bits = count.bit_length() - 1

    def gain_of(level):
        return 1.0 / math.sqrt(SPAN * 2 ** (level - 1) * HEAD)

    def weight_of(rows, level, h):
        at = (CBITS + level) * HEADS + h
        return weight_ref[rows, at : at + 1]

    def attend(c, h):
        rows = pl.ds(c * SPAN, SPAN)
        qs = qkv[rows, head_cols(h)]
        k = qkv[rows, head_cols(HEADS + h)]
        v = qkv[rows, head_cols(2 * HEADS + h)]
        scores = product(qs, k, ((1,), (1,)))
        probs = (scores * mix[c, h]).astype(jnp.bfloat16)
        got = product(probs, v, ((1,), (0,)))
        if c > 0:
            got += product(qs, first_sum[h], ((1,), (0,))) * (weight_of(rows, 1, h) * gain_of(1))
        acc[rows, head_cols(h)] = got

    def read(h):
        rows = pl.ds(0, count * SPAN)
        qs = qkv[:, head_cols(h)]
        got = acc[:, head_cols(h)]
        for bit in range(seq_bits):
            level = local_bits + bit + 1
            part = product(qs, left[bit, h], ((1,), (0,))) * (weight_of(rows, level, h) * gain_of(level))
            got += jnp.where(place.digit(bit) == 1, part, 0.0)
        attended[:, head_cols(h)] = got.astype(jnp.bfloat16)

    def project(near, tile):
        cols = pl.ds(tile * TILE, TILE)
        half = here // (seqs // 2)
        half = half if near else 1 - half
        deep = seqs // 2 * wo.rows
        w = wo_buf[pl.ds(half * (seqs // 2), seqs // 2), :, cols].reshape(deep, TILE)
        x = attended[:, pl.ds(pl.multiple_of(half * deep, 128), deep)]
        y = jnp.dot(x, w, preferred_element_type=jnp.float32)
        if near:
            total[:, cols] = y
        else:
            out_ref[:, cols] = (total[:, cols] + y).astype(out_ref.dtype)

    order = [(0, step) for step in range(1, last + 1)]
    split = max(last - APART, 0)
    order += [(n, step) for step in range(1, split + 1) for n in (1, 2)]
    order += [(n, step) for n in (1, 2) for step in range(split + 1, last + 1)]
    plan, end = [], {}
    for n, step in order:
        plan += [(n, step, group) for group in streams[n].groups(step)]
        end[n, step] = len(plan) - 1
    items = []

    def add(ready, cost, fn, *args):
        items.append((ready, cost, functools.partial(fn, *args)))

    for c in range(count):
        for h in range(HEADS):
            add(0, 1, mixing, c, h)
    done = {}
    for n, stream in enumerate(streams):
        for step in range(last + 1):
            done[n, step] = end[n, step] + LAG[n] + CLAG[n] if step else (end[0, last] + 1 if n else 0)
    ex_items = []

    def flush():
        while ex_items:
            ex_items.pop(0)[1]()

    for n, base in ((0, wide), (1, 0)):
        for step in range(last + 1):
            add(done[n, step], 0, streams[n].complete, step)
            for tile in range(streams[n].columns // TILE):
                add(done[n, step], 2 if streams[n].offsets(step)[1:] else 1, use, streams[n], base, step, tile)
        add(done[n, last], 0, at_once, streams[n], base)
        for h in range(HEADS) if n == 0 else ():
            add(done[n, last], 1, states, h)
    for h in range(HEADS):
        for c in range(count):
            add(done[1, last], 1, attend, c, h)
    for step in range(last + 1):
        add(done[2, step], 0, wo.complete, step)
    items.sort(key=lambda item: item[0])

    steps = [exchange_core, exchange_across] + [functools.partial(exchange_hop, b) for b in range(2, seq_bits)]
    at = done[0, last] + EX_FIRST
    for n, fn in enumerate(steps):
        ex_items.append((at + n * EX_LAG, fn))
        if n > 1:
            ex_items.append((at + n * EX_LAG + 1, functools.partial(exchange.collect, n - 1)))
    ex_items.append((at + (len(steps) - 1) * EX_LAG + 3, functools.partial(exchange.collect, seq_bits - 1)))
    for bit in range(1, seq_bits):
        ex_items.append((at + (len(steps) - 1) * EX_LAG + 5, functools.partial(exchange.finish, bit)))

    settles = {}
    for n, stream in enumerate(streams):
        for step in range(1, last + 1):
            settles.setdefault(end[n, step] + LAG[n], []).append(functools.partial(stream.settle, step))

    def run(tick, budget):
        for fn in settles.pop(tick, ()):
            fn()
        while ex_items and ex_items[0][0] <= tick and tick < len(plan):
            ready_at, fn = ex_items[0]
            if any(item[2].func is states or item[2].func is use and item[2].args[0] is kv for item in items):
                break
            ex_items.pop(0)
            fn()
        spent = 0
        while items and items[0][0] <= tick and (spent == 0 or spent + items[0][1] <= budget):
            _, cost, fn = items.pop(0)
            fn()
            spent += cost

    run(0, BEFORE)
    for tick, (n, step, group) in enumerate(plan):
        behind = (None if split else wo) if n else q
        for h, d in group:
            streams[n].arrive(step, h, d, behind)
        if tick == end[0, last]:
            q.begin_all()
            if split:
                wo.begin_all()
        if tick == end[1, last]:
            wo.begin_all()
        run(tick, BUDGET[n])
    late = sorted(settles)
    for tick in late[:-1]:
        for fn in settles[tick]:
            fn()
    tail = [fn for _, _, fn in items]
    ends = [fn for fn in tail if fn.func == wo.complete]
    for fn in tail:
        if fn not in ends:
            fn()
    for fn in settles[late[-1]] if late else ():
        fn()
    flush()
    for h in range(HEADS):
        read(h)
    tiles = range(wo.columns // TILE)
    for fn in ends[:-1]:
        fn()
    for tile in tiles:
        project(True, tile)
    ends[-1]()
    for tile in tiles:
        project(False, tile)
    for one in (*streams, exchange):
        one.drain()


def on_device(tokens, w_qkv, w_out, level_weight):
    groups, seqs = lax.axis_size("group"), lax.axis_size("seq")
    rows = tokens.shape[0]
    count = rows // SPAN
    seq_bits = seqs.bit_length() - 1
    wide = HEADS * HEAD
    square = (HEAD, HEAD)
    flat_rows = -(-level_weight.shape[0] * level_weight.shape[1] // 8) * 8
    vmem = pl.BlockSpec(memory_space=pltpu.VMEM)
    hbm = pl.BlockSpec(memory_space=pl.ANY)
    sems = pltpu.SemaphoreType.DMA((slots_needed(seqs),))
    return pl.pallas_call(
        functools.partial(layer_kernel, groups, seqs),
        out_shape=pltpu.VMEM((rows, w_out.shape[1]), jnp.bfloat16),
        in_specs=[hbm, hbm, hbm, hbm],
        out_specs=vmem,
        scratch_shapes=[
            pltpu.VMEM(tokens.shape, jnp.bfloat16),
            pltpu.VMEM((seqs, w_qkv.shape[0], 2 * wide), jnp.bfloat16),
            pltpu.VMEM((seqs, w_qkv.shape[0], wide), jnp.bfloat16),
            pltpu.VMEM((seqs, *w_out.shape), jnp.bfloat16),
            pltpu.VMEM((rows, w_qkv.shape[1]), jnp.float32),
            pltpu.VMEM((rows, w_qkv.shape[1]), jnp.bfloat16),
            pltpu.VMEM((count, HEADS, SPAN, SPAN), jnp.float32),
            pltpu.VMEM((rows, wide), jnp.float32),
            pltpu.VMEM((rows, wide), jnp.bfloat16),
            pltpu.VMEM(level_weight.shape, jnp.float32),
            pltpu.VMEM((flat_rows, rows), jnp.float32),
            pltpu.VMEM((rows, flat_rows), jnp.float32),
            pltpu.VMEM((HEADS, *square), jnp.float32),
            pltpu.VMEM((HEADS, *square), jnp.bfloat16),
            pltpu.VMEM((HEADS, *square), jnp.bfloat16),
            pltpu.VMEM((2, *square), jnp.float32),
            pltpu.VMEM((2, *square), jnp.bfloat16),
            pltpu.VMEM((seq_bits, *square), jnp.bfloat16),
            pltpu.VMEM((seq_bits, HEADS, *square), jnp.bfloat16),
            pltpu.SemaphoreType.DMA((5,)),
            *[sems] * 6,
            pltpu.SemaphoreType.DMA((8 * seq_bits,)),
            pltpu.SemaphoreType.DMA((8 * seq_bits,)),
        ],
        compiler_params=pltpu.CompilerParams(
            collective_id=0, has_side_effects=True, vmem_limit_bytes=58 * 1024 * 1024
        ),
    )(tokens, w_qkv, w_out, level_weight)


def solution(mesh):
    return jax.shard_map(
        on_device,
        mesh=mesh,
        in_specs=(
            P(("group", "seq"), None),
            P("seq", None),
            P("seq", None),
            P(None, None, ("group", "seq")),
        ),
        out_specs=P(("group", "seq"), None),
        check_vma=False,
    )
```

```python
import functools
import math

import jax
import jax.numpy as jnp
from jax import lax
from jax.experimental import pallas as pl
from jax.experimental.pallas import tpu as pltpu
from jax.sharding import PartitionSpec as P

HEADS = 4
HEAD = 256
SPAN = 256
CBITS = 8
TILE = 512
MESH = pl.DeviceIdType.MESH
PIECES = (4, 4, 4)
SHARE = ((5, 6, 6, 6), (4, 6, 6, 6), (5, 6, 6, 6))
LAG = (2, 5, 5)
CLAG = (1, 2, 2)
BUDGET = (4, 3, 3)
EX_FIRST = 4
EX_LAG = 6
APART = 1
BEFORE = 8


class Place:
    def __init__(self, groups, seqs):
        self.seqs = seqs
        self.chips = seqs // 2
        self.has_x = groups % 2 == 0
        self.g = lax.axis_index("group")
        self.me = lax.axis_index("seq")
        self.core = lax.rem(self.me, 2)
        self.chip = self.me // 2
        odd = lax.rem(self.chip, 2)
        half = self.chip // 2
        self.pos = half + odd * (self.chips - 1 - 2 * half)
        self.par = lax.rem(self.g, 2)
        self.mate = (self.g, self.me + 1 - 2 * self.core)
        self.cross = (self.g + 1 - 2 * self.par, self.me)

    def chip_at(self, offset):
        pos = lax.rem(self.pos + offset + self.chips, self.chips)
        late = pos // (self.chips // 2)
        return 2 * pos + late * (2 * (self.chips - 1) + 1 - 4 * pos)

    def ring(self, offset):
        return (self.g, self.chip_at(offset) * 2 + self.core)

    def flip(self, bit):
        return (self.g, self.me + (1 - 2 * self.digit(bit)) * 2**bit)

    def aslant(self, bit):
        return (self.g, self.flip(bit)[1] + (1 - 2 * self.digit(1)) * 2)

    def digit(self, bit):
        return lax.rem(self.me // 2**bit, 2)

    def greet(self, others):
        barrier = pltpu.get_barrier_semaphore()
        for other in others:
            pl.semaphore_signal(barrier, inc=1, device_id=other, device_id_type=MESH)
        pl.semaphore_wait(barrier, len(others))

    def neighbours(self):
        found = [self.ring(1), self.ring(-1), self.mate]
        return found + [self.cross] if self.has_x else found


class Gather:
    def __init__(self, place, buf, pieces, share, send_sem, recv_sem):
        self.at, self.buf = place, buf
        self.send_sem, self.recv_sem = send_sem, recv_sem
        _, self.rows, self.columns = buf.shape
        self.pieces = max(1, min(pieces, self.rows // 16))
        self.part = self.rows // self.pieces
        self.share = share
        self.every = (0, self.columns)
        self.last = place.chips // 2
        self.slots, self.sent = {}, {}
        self.waiting = {}
        for d in self.directions(1):
            self.waiting[d] = self.turn(1, d)

    def rel(self, step):
        share = self.share[(step - 1) * len(self.share) // self.last]
        return (self.columns * share // 16) // 128 * 128 if self.at.has_x else 0

    def ring_cols(self, step):
        rel = self.rel(step)
        return (self.at.par * rel if rel else 0, self.columns - rel)

    def give_cols(self, step):
        return (self.at.par * (self.columns - self.rel(step)), self.rel(step))

    def take_cols(self, step):
        return ((1 - self.at.par) * (self.columns - self.rel(step)), self.rel(step))

    def mine(self, offset):
        return self.at.chip_at(offset) * 2 + self.at.core

    def theirs(self, offset):
        return self.at.chip_at(offset) * 2 + 1 - self.at.core

    def span(self, step, d):
        if step < self.last:
            return (0, self.pieces)
        half = self.pieces // 2
        if d == 1:
            return (0, max(half, 1))
        return (half, half)

    def directions(self, step):
        return [d for d in (1, -1) if self.span(step, d)[1]]

    def turn(self, step, d):
        first, count = self.span(step, d)
        start = self.span(self.last, d)[0] - first
        return [first + (start + n) % count for n in range(count)]

    def groups(self, step):
        turns = [[(h, d) for h in self.turn(step, d)] for d in self.directions(step)]
        return list(zip(*turns))

    def copy(self, sent, got, index, rows, cols, device):
        start, width = cols
        if not isinstance(start, int):
            start = pl.multiple_of(start, 128)
        first, count = rows
        ref = self.buf.at[index, pl.ds(first * self.part, count * self.part), pl.ds(start, width)]
        return pltpu.make_async_remote_copy(
            src_ref=ref,
            dst_ref=ref,
            send_sem=self.send_sem.at[self.slots.setdefault(("send", *sent), len(self.slots))],
            recv_sem=self.recv_sem.at[self.slots.setdefault(("recv", *got), len(self.slots))],
            device_id=device,
            device_id_type=MESH,
        )

    def send(self, sent, got, index, rows, cols, device):
        self.copy(sent, got, index, rows, cols, device).start()
        before = self.sent.get(sent, (0, cols, device))
        self.sent[sent] = (before[0] + rows[1], cols, device)

    def ring_send(self, step, h, d):
        index = self.mine(-d * (step - 1))
        self.send(("ring", step, d), ("ring", step, d, h), index, (h, 1), self.ring_cols(step), self.at.ring(d))

    def begin(self, d):
        left = self.waiting.get(d)
        if left:
            self.ring_send(1, left.pop(0), d)

    def begin_all(self):
        for _ in range(self.pieces):
            for d in (1, -1):
                self.begin(d)

    def own(self):
        key = ("mate", 0, 1)
        self.send(key, key, self.at.me, (0, self.pieces), self.every, self.at.mate)

    def arrive(self, step, h, d, behind):
        index = self.mine(-d * step)
        key = ("ring", step, d)
        self.copy(key, (*key, h), index, (h, 1), self.ring_cols(step), self.at.ring(-d)).wait_recv()
        first, count = self.span(step + 1, d) if step < self.last else (0, 0)
        if first <= h < first + count:
            self.ring_send(step + 1, h, d)
        elif behind:
            behind.begin(d)
        if self.rel(step):
            key = ("cross", step, d)
            self.send(key, key, index, (h, 1), self.give_cols(step), self.at.cross)

    def settle(self, step):
        for d in self.directions(step):
            index = self.mine(-d * step)
            rows = self.span(step, d)
            if self.rel(step):
                key = ("cross", step, d)
                self.copy(key, key, index, rows, self.take_cols(step), self.at.cross).wait_recv()
            key = ("mate", step, d)
            self.send(key, key, index, rows, self.every, self.at.mate)

    def complete(self, step):
        for d in self.directions(step) if step else (1,):
            key = ("mate", step, d)
            rows = self.span(step, d) if step else (0, self.pieces)
            self.copy(key, key, self.theirs(-d * step), rows, self.every, self.at.mate).wait_recv()

    def offsets(self, step):
        return (step, -step) if 0 < step < self.last else (step,)

    def drain(self, keep=()):
        for sent, (count, cols, device) in list(self.sent.items()):
            if sent[1] not in keep:
                self.copy(sent, sent, 0, (0, count), cols, device).wait_send()
                del self.sent[sent]


def slots_needed(seqs):
    return (seqs // 4) * 20 + 8


class Exchange:
    def __init__(self, place, left, bits, send_sem, recv_sem):
        self.at, self.left, self.bits = place, left, bits
        self.send_sem, self.recv_sem = send_sem, recv_sem
        self.slots, self.sent = {}, []
        self.c, self.y = place.core, place.digit(1)
        self.head = 2 * self.c + self.y
        self.other = 2 * self.c + 1 - self.y
        self.mate_head = 2 * (1 - self.c) + self.y
        self.mate_other = 2 * (1 - self.c) + 1 - self.y

    def copy(self, key, src, bit, head, device):
        slot = self.slots.setdefault(key, len(self.slots))
        return pltpu.make_async_remote_copy(
            src_ref=src,
            dst_ref=self.left.at[bit, head],
            send_sem=self.send_sem.at[slot],
            recv_sem=self.recv_sem.at[slot],
            device_id=device,
            device_id_type=MESH,
        )

    def reads(self, bit):
        return self.at.digit(bit) == 1

    def end(self):
        return self.at.me // 4 == self.at.seqs // 4 - 1

    def send(self, when, *args):
        self.sent.append((when, args))
        guarded(when, lambda: self.copy(*args).start())

    def forward(self, when, key, bit, head, device):
        self.send(when, key, self.left.at[bit, head], bit, head, device)

    def wait(self, when, key, bit, head, device):
        guarded(when, lambda: self.copy(key, self.left.at[bit, head], bit, head, device).wait_recv())

    def hop(self, bit, src):
        top = bit == self.bits - 1
        self.send(self.at.digit(bit) == 0 if top else None, ("hop", bit), src, bit, self.head, self.at.flip(bit))
        if top:
            near_end = self.at.me // 4 == self.at.seqs // 4 - 1 - 2**bit // 4
            self.send(near_end, ("diag", bit), src, bit, self.head, self.at.aslant(bit))

    def hopped(self, bit):
        top = bit == self.bits - 1
        self.wait(self.reads(bit) if top else None, ("hop", bit), bit, self.head, self.at.flip(bit))

    def spread(self, bit):
        reads = self.reads(bit)
        if bit > 1:
            quad = jnp.logical_and(reads, jnp.logical_not(self.end())) if bit == self.bits - 1 else reads
            self.forward(quad, ("quad", bit), bit, self.head, self.at.flip(1))
        self.forward(reads, ("near", bit), bit, self.head, self.at.mate)

    def collect(self, bit):
        reads = self.reads(bit)
        if bit == 1:
            self.wait(reads, ("across", 1), bit, self.other, self.at.flip(1))
        elif bit == self.bits - 1:
            quad = jnp.logical_and(reads, jnp.logical_not(self.end()))
            self.wait(quad, ("quad", bit), bit, self.other, self.at.flip(1))
            self.wait(self.end(), ("diag", bit), bit, self.other, self.at.aslant(bit))
        else:
            self.wait(reads, ("quad", bit), bit, self.other, self.at.flip(1))
        self.forward(reads, ("far", bit), bit, self.other, self.at.mate)

    def finish(self, bit):
        self.wait(self.reads(bit), ("near", bit), bit, self.mate_head, self.at.mate)
        self.wait(self.reads(bit), ("far", bit), bit, self.mate_other, self.at.mate)

    def drain(self):
        for when, args in self.sent:
            guarded(when, lambda: self.copy(*args).wait_send())


def guarded(when, fn):
    if when is None:
        fn()
    else:
        pl.when(when)(fn)


def product(a, b, dims):
    return lax.dot_general(a, b, (dims, ((), ())), preferred_element_type=jnp.float32)


def head_cols(h):
    return pl.ds(h * HEAD, HEAD)


def layer_kernel(
    groups, seqs, tokens_hbm, w_ref, wo_ref, lw_hbm, out_ref,
    tokens_ref, kv_buf, q_buf, wo_buf, total, qkv, mix, acc, attended, lw_ref, flat, weight_ref, local_sum, first_sum, give, pair,
    pair_give, run_give, left, load_sem, kv_send, kv_recv, q_send, q_recv, wo_send, wo_recv, ex_send, ex_recv,
):
    place = Place(groups, seqs)
    rows_w, columns = w_ref.shape
    wide = HEADS * HEAD
    here = place.me
    loads = [
        pltpu.make_async_copy(src, dst, load_sem.at[n])
        for n, (src, dst) in enumerate(
            (
                (w_ref.at[:, pl.ds(wide, columns - wide)], kv_buf.at[here]),
                (w_ref.at[:, pl.ds(0, wide)], q_buf.at[here]),
                (wo_ref, wo_buf.at[here]),
                (lw_hbm, lw_ref),
                (tokens_hbm, tokens_ref),
            )
        )
    ]
    for one in loads:
        one.start()
    seq_bits = seqs.bit_length() - 1
    place.greet(place.neighbours() + [place.flip(b) for b in range(1, seq_bits)] + [place.aslant(seq_bits - 1)])
    kv = Gather(place, kv_buf, PIECES[0], SHARE[0], kv_send, kv_recv)
    q = Gather(place, q_buf, PIECES[1], SHARE[1], q_send, q_recv)
    wo = Gather(place, wo_buf, PIECES[2], SHARE[2], wo_send, wo_recv)
    streams = (kv, q, wo)
    last = kv.last
    loads[0].wait()
    kv.begin_all()
    kv.own()
    for one in loads[1:]:
        one.wait()
    for stream in streams[1:]:
        stream.own()

    count = tokens_ref.shape[0] // SPAN
    levels, heads, tokens_here = lw_ref.shape

    for level in range(levels):
        flat[level * heads : (level + 1) * heads, :] = lw_ref[level]
    spare = flat.shape[0] - levels * heads
    if spare:
        flat[levels * heads :, :] = jnp.zeros((spare, tokens_here), jnp.float32)
    weight_ref[...] = flat[...].T

    def mixing(c, h):
        rows = pl.ds(c * SPAN, SPAN)
        i = lax.broadcasted_iota(jnp.int32, (SPAN, SPAN), 0)
        j = lax.broadcasted_iota(jnp.int32, (SPAN, SPAN), 1)
        apart = i ^ j
        value = jnp.zeros((SPAN, SPAN), jnp.float32)
        for level in range(CBITS + 1):
            gain = 1.0 / math.sqrt(HEAD * max(1, 2 ** (level - 1)))
            column = weight_ref[rows, level * HEADS + h : level * HEADS + h + 1] * gain
            column = jnp.broadcast_to(column, (SPAN, SPAN))
            value = column if level == 0 else jnp.where(apart >= 2 ** (level - 1), column, value)
        mix[c, h] = jnp.where(i >= j, value, 0.0)

    aligned = (2 * rows_w) % 128 == 0

    def use(stream, base, step, tile):
        if not aligned:
            return
        cols = pl.ds(tile * TILE, TILE)
        y = None
        for offset in stream.offsets(step):
            chip = place.chip_at(offset)
            x = tokens_ref[:, pl.ds(pl.multiple_of(chip * (2 * rows_w), 128), 2 * rows_w)]
            w = stream.buf[pl.ds(chip * 2, 2), :, cols].reshape(2 * rows_w, TILE)
            part = jnp.dot(x, w, preferred_element_type=jnp.float32)
            y = part if y is None else y + part
        if step:
            y = total[:, pl.ds(base + tile * TILE, TILE)] + y
        if step < last:
            total[:, pl.ds(base + tile * TILE, TILE)] = y
        else:
            qkv[:, pl.ds(base + tile * TILE, TILE)] = y.astype(qkv.dtype)

    def at_once(stream, base):
        if aligned:
            return

        @pl.loop(0, stream.columns // TILE)
        def _(t):
            cols = pl.ds(pl.multiple_of(t * TILE, TILE), TILE)
            w = stream.buf[:, :, cols].reshape(seqs * rows_w, TILE)
            y = jnp.dot(tokens_ref[...], w, preferred_element_type=jnp.float32)
            qkv[:, pl.ds(pl.multiple_of(base + t * TILE, TILE), TILE)] = y.astype(qkv.dtype)

    exchange = Exchange(place, left, seq_bits, ex_send, ex_recv)

    def states(h):
        for c in range(count):
            k = qkv[pl.ds(c * SPAN, SPAN), head_cols(HEADS + h)]
            v = qkv[pl.ds(c * SPAN, SPAN), head_cols(2 * HEADS + h)]
            state = product(k, v, ((0,), (0,)))
            if c == 0:
                local_sum[h] = state
                first_sum[h] = state.astype(jnp.bfloat16)
            else:
                local_sum[h] += state
        give[h] = local_sum[h].astype(jnp.bfloat16)
        exchange.send(None, ("core", h), give.at[h], 0, h, place.mate)

    running = {}

    def exchange_core():
        for h in range(HEADS):
            exchange.wait(None, ("core", h), 0, h, place.mate)
        for n in range(2):
            h = 2 * place.core + n
            pair[n] = local_sum[h] + left[0, h].astype(jnp.float32)
            pair_give[n] = pair[n].astype(jnp.bfloat16)
        y = place.digit(1)
        for n, which in enumerate((1 - y, y)):
            exchange.send(y == 0 if n else None, ("across", n), pair_give.at[which], 1, 2 * place.core + which, place.flip(1))

    def exchange_across():
        y = place.digit(1)
        exchange.wait(None, ("across", 0), 1, exchange.head, place.flip(1))
        pair[0] = pair[y] + left[1, exchange.head].astype(jnp.float32)
        run_give[2] = pair[0].astype(jnp.bfloat16)
        exchange.hop(2, run_give.at[2])
        exchange.spread(1)

    def exchange_hop(bit):
        exchange.hopped(bit)
        if bit + 1 < seq_bits:
            pair[0] += left[bit, exchange.head].astype(jnp.float32)
            run_give[bit + 1] = pair[0].astype(jnp.bfloat16)
            exchange.hop(bit + 1, run_give.at[bit + 1])
        exchange.spread(bit)

    local_bits = count.bit_length() - 1

    def gain_of(level):
        return 1.0 / math.sqrt(SPAN * 2 ** (level - 1) * HEAD)

    def weight_of(rows, level, h):
        at = (CBITS + level) * HEADS + h
        return weight_ref[rows, at : at + 1]

    def attend(c, h):
        rows = pl.ds(c * SPAN, SPAN)
        qs = qkv[rows, head_cols(h)]
        k = qkv[rows, head_cols(HEADS + h)]
        v = qkv[rows, head_cols(2 * HEADS + h)]
        scores = product(qs, k, ((1,), (1,)))
        probs = (scores * mix[c, h]).astype(jnp.bfloat16)
        got = product(probs, v, ((1,), (0,)))
        if c > 0:
            got += product(qs, first_sum[h], ((1,), (0,))) * (weight_of(rows, 1, h) * gain_of(1))
        acc[rows, head_cols(h)] = got

    def read(h):
        rows = pl.ds(0, count * SPAN)
        qs = qkv[:, head_cols(h)]
        got = acc[:, head_cols(h)]
        for bit in range(seq_bits):
            level = local_bits + bit + 1
            part = product(qs, left[bit, h], ((1,), (0,))) * (weight_of(rows, level, h) * gain_of(level))
            got += jnp.where(place.digit(bit) == 1, part, 0.0)
        attended[:, head_cols(h)] = got.astype(jnp.bfloat16)

    def project(near, tile):
        cols = pl.ds(tile * TILE, TILE)
        half = here // (seqs // 2)
        half = half if near else 1 - half
        deep = seqs // 2 * wo.rows
        w = wo_buf[pl.ds(half * (seqs // 2), seqs // 2), :, cols].reshape(deep, TILE)
        x = attended[:, pl.ds(pl.multiple_of(half * deep, 128), deep)]
        y = jnp.dot(x, w, preferred_element_type=jnp.float32)
        if near:
            total[:, cols] = y
        else:
            out_ref[:, cols] = (total[:, cols] + y).astype(out_ref.dtype)

    order = [(0, step) for step in range(1, last + 1)]
    split = max(last - APART, 0)
    order += [(n, step) for step in range(1, split + 1) for n in (1, 2)]
    order += [(n, step) for n in (1, 2) for step in range(split + 1, last + 1)]
    plan, end = [], {}
    for n, step in order:
        plan += [(n, step, group) for group in streams[n].groups(step)]
        end[n, step] = len(plan) - 1
    items = []

    def add(ready, cost, fn, *args):
        items.append((ready, cost, functools.partial(fn, *args)))

    for c in range(count):
        for h in range(HEADS):
            add(0, 1, mixing, c, h)
    done = {}
    for n, stream in enumerate(streams):
        for step in range(last + 1):
            done[n, step] = end[n, step] + LAG[n] + CLAG[n] if step else (end[0, last] + 1 if n else 0)
    ex_items = []

    def flush():
        while ex_items:
            ex_items.pop(0)[1]()

    for n, base in ((0, wide), (1, 0)):
        for step in range(last + 1):
            add(done[n, step], 0, streams[n].complete, step)
            for tile in range(streams[n].columns // TILE):
                add(done[n, step], 2 if streams[n].offsets(step)[1:] else 1, use, streams[n], base, step, tile)
        add(done[n, last], 0, at_once, streams[n], base)
        for h in range(HEADS) if n == 0 else ():
            add(done[n, last], 1, states, h)
    for h in range(HEADS):
        for c in range(count):
            add(done[1, last], 1, attend, c, h)
    for step in range(last + 1):
        add(done[2, step], 0, wo.complete, step)
    add(min(done[0, last] + 8, len(plan) - 1), 0, kv.drain)
    for stream in (q, wo):
        add(len(plan) - 1, 0, stream.drain, (last - 1, last))
    items.sort(key=lambda item: item[0])

    steps = [exchange_core, exchange_across] + [functools.partial(exchange_hop, b) for b in range(2, seq_bits)]
    at = done[0, last] + EX_FIRST
    for n, fn in enumerate(steps):
        ex_items.append((at + n * EX_LAG, fn))
        if n > 1:
            ex_items.append((at + n * EX_LAG + 1, functools.partial(exchange.collect, n - 1)))
    ex_items.append((at + (len(steps) - 1) * EX_LAG + 3, functools.partial(exchange.collect, seq_bits - 1)))
    for bit in range(1, seq_bits):
        ex_items.append((at + (len(steps) - 1) * EX_LAG + 5, functools.partial(exchange.finish, bit)))

    settles = {}
    for n, stream in enumerate(streams):
        for step in range(1, last + 1):
            settles.setdefault(end[n, step] + LAG[n], []).append(functools.partial(stream.settle, step))

    def run(tick, budget):
        for fn in settles.pop(tick, ()):
            fn()
        while ex_items and ex_items[0][0] <= tick and tick < len(plan):
            ready_at, fn = ex_items[0]
            if any(item[2].func is states or item[2].func is use and item[2].args[0] is kv for item in items):
                break
            ex_items.pop(0)
            fn()
        spent = 0
        while items and items[0][0] <= tick and (spent == 0 or spent + items[0][1] <= budget):
            _, cost, fn = items.pop(0)
            fn()
            spent += cost

    run(0, BEFORE)
    for tick, (n, step, group) in enumerate(plan):
        behind = (None if split else wo) if n else q
        for h, d in group:
            streams[n].arrive(step, h, d, behind)
        if tick == end[0, last]:
            q.begin_all()
            if split:
                wo.begin_all()
        if tick == end[1, last]:
            wo.begin_all()
        run(tick, BUDGET[n])
    late = sorted(settles)
    for tick in late[:-1]:
        for fn in settles[tick]:
            fn()
    tail = [fn for _, _, fn in items]
    ends = [fn for fn in tail if fn.func == wo.complete]
    for fn in tail:
        if fn not in ends:
            fn()
    for fn in settles[late[-1]] if late else ():
        fn()
    flush()
    for h in range(HEADS):
        read(h)
    tiles = range(wo.columns // TILE)
    for fn in ends[:-1]:
        fn()
    for tile in tiles:
        project(True, tile)
    ends[-1]()
    for tile in tiles:
        project(False, tile)
    for one in (*streams, exchange):
        one.drain()


def on_device(tokens, w_qkv, w_out, level_weight):
    groups, seqs = lax.axis_size("group"), lax.axis_size("seq")
    rows = tokens.shape[0]
    count = rows // SPAN
    seq_bits = seqs.bit_length() - 1
    wide = HEADS * HEAD
    square = (HEAD, HEAD)
    flat_rows = -(-level_weight.shape[0] * level_weight.shape[1] // 8) * 8
    vmem = pl.BlockSpec(memory_space=pltpu.VMEM)
    hbm = pl.BlockSpec(memory_space=pl.ANY)
    sems = pltpu.SemaphoreType.DMA((slots_needed(seqs),))
    return pl.pallas_call(
        functools.partial(layer_kernel, groups, seqs),
        out_shape=pltpu.VMEM((rows, w_out.shape[1]), jnp.bfloat16),
        in_specs=[hbm, hbm, hbm, hbm],
        out_specs=vmem,
        scratch_shapes=[
            pltpu.VMEM(tokens.shape, jnp.bfloat16),
            pltpu.VMEM((seqs, w_qkv.shape[0], 2 * wide), jnp.bfloat16),
            pltpu.VMEM((seqs, w_qkv.shape[0], wide), jnp.bfloat16),
            pltpu.VMEM((seqs, *w_out.shape), jnp.bfloat16),
            pltpu.VMEM((rows, w_qkv.shape[1]), jnp.float32),
            pltpu.VMEM((rows, w_qkv.shape[1]), jnp.bfloat16),
            pltpu.VMEM((count, HEADS, SPAN, SPAN), jnp.float32),
            pltpu.VMEM((rows, wide), jnp.float32),
            pltpu.VMEM((rows, wide), jnp.bfloat16),
            pltpu.VMEM(level_weight.shape, jnp.float32),
            pltpu.VMEM((flat_rows, rows), jnp.float32),
            pltpu.VMEM((rows, flat_rows), jnp.float32),
            pltpu.VMEM((HEADS, *square), jnp.float32),
            pltpu.VMEM((HEADS, *square), jnp.bfloat16),
            pltpu.VMEM((HEADS, *square), jnp.bfloat16),
            pltpu.VMEM((2, *square), jnp.float32),
            pltpu.VMEM((2, *square), jnp.bfloat16),
            pltpu.VMEM((seq_bits, *square), jnp.bfloat16),
            pltpu.VMEM((seq_bits, HEADS, *square), jnp.bfloat16),
            pltpu.SemaphoreType.DMA((5,)),
            *[sems] * 6,
            pltpu.SemaphoreType.DMA((8 * seq_bits,)),
            pltpu.SemaphoreType.DMA((8 * seq_bits,)),
        ],
        compiler_params=pltpu.CompilerParams(
            collective_id=0, has_side_effects=True, vmem_limit_bytes=58 * 1024 * 1024
        ),
    )(tokens, w_qkv, w_out, level_weight)


def solution(mesh):
    return jax.shard_map(
        on_device,
        mesh=mesh,
        in_specs=(
            P(("group", "seq"), None),
            P("seq", None),
            P("seq", None),
            P(None, None, ("group", "seq")),
        ),
        out_specs=P(("group", "seq"), None),
        check_vma=False,
    )
```

```python
import functools
import math

import jax
import jax.numpy as jnp
from jax import lax
from jax.experimental import pallas as pl
from jax.experimental.pallas import tpu as pltpu
from jax.sharding import PartitionSpec as P

HEADS = 4
HEAD = 256
SPAN = 256
CBITS = 8
TILE = 512
MESH = pl.DeviceIdType.MESH
PIECES = (4, 4, 4)
SHARE = ((5, 6, 6, 6), (4, 6, 6, 6), (5, 6, 6, 6))
LAG = (2, 5, 5)
CLAG = (1, 2, 2)
BUDGET = (4, 3, 3)
EX_FIRST = 4
EX_LAG = 6
APART = 1
BEFORE = 12


class Place:
    def __init__(self, groups, seqs):
        self.seqs = seqs
        self.chips = seqs // 2
        self.has_x = groups % 2 == 0
        self.g = lax.axis_index("group")
        self.me = lax.axis_index("seq")
        self.core = lax.rem(self.me, 2)
        self.chip = self.me // 2
        odd = lax.rem(self.chip, 2)
        half = self.chip // 2
        self.pos = half + odd * (self.chips - 1 - 2 * half)
        self.par = lax.rem(self.g, 2)
        self.mate = (self.g, self.me + 1 - 2 * self.core)
        self.cross = (self.g + 1 - 2 * self.par, self.me)

    def chip_at(self, offset):
        pos = lax.rem(self.pos + offset + self.chips, self.chips)
        late = pos // (self.chips // 2)
        return 2 * pos + late * (2 * (self.chips - 1) + 1 - 4 * pos)

    def ring(self, offset):
        return (self.g, self.chip_at(offset) * 2 + self.core)

    def flip(self, bit):
        return (self.g, self.me + (1 - 2 * self.digit(bit)) * 2**bit)

    def aslant(self, bit):
        return (self.g, self.flip(bit)[1] + (1 - 2 * self.digit(1)) * 2)

    def digit(self, bit):
        return lax.rem(self.me // 2**bit, 2)

    def greet(self, others):
        barrier = pltpu.get_barrier_semaphore()
        for other in others:
            pl.semaphore_signal(barrier, inc=1, device_id=other, device_id_type=MESH)
        pl.semaphore_wait(barrier, len(others))

    def neighbours(self):
        found = [self.ring(1), self.ring(-1), self.mate]
        return found + [self.cross] if self.has_x else found


class Gather:
    def __init__(self, place, buf, pieces, share, send_sem, recv_sem):
        self.at, self.buf = place, buf
        self.send_sem, self.recv_sem = send_sem, recv_sem
        _, self.rows, self.columns = buf.shape
        self.pieces = max(1, min(pieces, self.rows // 16))
        self.part = self.rows // self.pieces
        self.share = share
        self.every = (0, self.columns)
        self.last = place.chips // 2
        self.slots, self.sent = {}, {}
        self.waiting = {}
        for d in self.directions(1):
            self.waiting[d] = self.turn(1, d)

    def rel(self, step):
        share = self.share[(step - 1) * len(self.share) // self.last]
        return (self.columns * share // 16) // 128 * 128 if self.at.has_x else 0

    def ring_cols(self, step):
        rel = self.rel(step)
        return (self.at.par * rel if rel else 0, self.columns - rel)

    def give_cols(self, step):
        return (self.at.par * (self.columns - self.rel(step)), self.rel(step))

    def take_cols(self, step):
        return ((1 - self.at.par) * (self.columns - self.rel(step)), self.rel(step))

    def mine(self, offset):
        return self.at.chip_at(offset) * 2 + self.at.core

    def theirs(self, offset):
        return self.at.chip_at(offset) * 2 + 1 - self.at.core

    def span(self, step, d):
        if step < self.last:
            return (0, self.pieces)
        half = self.pieces // 2
        if d == 1:
            return (0, max(half, 1))
        return (half, half)

    def directions(self, step):
        return [d for d in (1, -1) if self.span(step, d)[1]]

    def turn(self, step, d):
        first, count = self.span(step, d)
        start = self.span(self.last, d)[0] - first
        return [first + (start + n) % count for n in range(count)]

    def groups(self, step):
        turns = [[(h, d) for h in self.turn(step, d)] for d in self.directions(step)]
        return list(zip(*turns))

    def copy(self, sent, got, index, rows, cols, device):
        start, width = cols
        if not isinstance(start, int):
            start = pl.multiple_of(start, 128)
        first, count = rows
        ref = self.buf.at[index, pl.ds(first * self.part, count * self.part), pl.ds(start, width)]
        return pltpu.make_async_remote_copy(
            src_ref=ref,
            dst_ref=ref,
            send_sem=self.send_sem.at[self.slots.setdefault(("send", *sent), len(self.slots))],
            recv_sem=self.recv_sem.at[self.slots.setdefault(("recv", *got), len(self.slots))],
            device_id=device,
            device_id_type=MESH,
        )

    def send(self, sent, got, index, rows, cols, device):
        self.copy(sent, got, index, rows, cols, device).start()
        before = self.sent.get(sent, (0, cols, device))
        self.sent[sent] = (before[0] + rows[1], cols, device)

    def ring_send(self, step, h, d):
        index = self.mine(-d * (step - 1))
        self.send(("ring", step, d), ("ring", step, d, h), index, (h, 1), self.ring_cols(step), self.at.ring(d))

    def begin(self, d):
        left = self.waiting.get(d)
        if left:
            self.ring_send(1, left.pop(0), d)

    def begin_all(self):
        for _ in range(self.pieces):
            for d in (1, -1):
                self.begin(d)

    def own(self):
        key = ("mate", 0, 1)
        self.send(key, key, self.at.me, (0, self.pieces), self.every, self.at.mate)

    def arrive(self, step, h, d, behind):
        index = self.mine(-d * step)
        key = ("ring", step, d)
        self.copy(key, (*key, h), index, (h, 1), self.ring_cols(step), self.at.ring(-d)).wait_recv()
        first, count = self.span(step + 1, d) if step < self.last else (0, 0)
        if first <= h < first + count:
            self.ring_send(step + 1, h, d)
        elif behind:
            behind.begin(d)
        if self.rel(step):
            key = ("cross", step, d)
            self.send(key, key, index, (h, 1), self.give_cols(step), self.at.cross)

    def settle(self, step):
        for d in self.directions(step):
            index = self.mine(-d * step)
            rows = self.span(step, d)
            if self.rel(step):
                key = ("cross", step, d)
                self.copy(key, key, index, rows, self.take_cols(step), self.at.cross).wait_recv()
            key = ("mate", step, d)
            self.send(key, key, index, rows, self.every, self.at.mate)

    def complete(self, step):
        for d in self.directions(step) if step else (1,):
            key = ("mate", step, d)
            rows = self.span(step, d) if step else (0, self.pieces)
            self.copy(key, key, self.theirs(-d * step), rows, self.every, self.at.mate).wait_recv()

    def offsets(self, step):
        return (step, -step) if 0 < step < self.last else (step,)

    def drain(self, keep=()):
        for sent, (count, cols, device) in list(self.sent.items()):
            if sent[1] not in keep:
                self.copy(sent, sent, 0, (0, count), cols, device).wait_send()
                del self.sent[sent]


def slots_needed(seqs):
    return (seqs // 4) * 20 + 8


class Exchange:
    def __init__(self, place, left, bits, send_sem, recv_sem):
        self.at, self.left, self.bits = place, left, bits
        self.send_sem, self.recv_sem = send_sem, recv_sem
        self.slots, self.sent = {}, []
        self.c, self.y = place.core, place.digit(1)
        self.head = 2 * self.c + self.y
        self.other = 2 * self.c + 1 - self.y
        self.mate_head = 2 * (1 - self.c) + self.y
        self.mate_other = 2 * (1 - self.c) + 1 - self.y

    def copy(self, key, src, bit, head, device):
        slot = self.slots.setdefault(key, len(self.slots))
        return pltpu.make_async_remote_copy(
            src_ref=src,
            dst_ref=self.left.at[bit, head],
            send_sem=self.send_sem.at[slot],
            recv_sem=self.recv_sem.at[slot],
            device_id=device,
            device_id_type=MESH,
        )

    def reads(self, bit):
        return self.at.digit(bit) == 1

    def end(self):
        return self.at.me // 4 == self.at.seqs // 4 - 1

    def send(self, when, *args):
        self.sent.append((when, args))
        guarded(when, lambda: self.copy(*args).start())

    def forward(self, when, key, bit, head, device):
        self.send(when, key, self.left.at[bit, head], bit, head, device)

    def wait(self, when, key, bit, head, device):
        guarded(when, lambda: self.copy(key, self.left.at[bit, head], bit, head, device).wait_recv())

    def hop(self, bit, src):
        top = bit == self.bits - 1
        self.send(self.at.digit(bit) == 0 if top else None, ("hop", bit), src, bit, self.head, self.at.flip(bit))
        if top:
            near_end = self.at.me // 4 == self.at.seqs // 4 - 1 - 2**bit // 4
            self.send(near_end, ("diag", bit), src, bit, self.head, self.at.aslant(bit))

    def hopped(self, bit):
        top = bit == self.bits - 1
        self.wait(self.reads(bit) if top else None, ("hop", bit), bit, self.head, self.at.flip(bit))

    def spread(self, bit):
        reads = self.reads(bit)
        if bit > 1:
            quad = jnp.logical_and(reads, jnp.logical_not(self.end())) if bit == self.bits - 1 else reads
            self.forward(quad, ("quad", bit), bit, self.head, self.at.flip(1))
        self.forward(reads, ("near", bit), bit, self.head, self.at.mate)

    def collect(self, bit):
        reads = self.reads(bit)
        if bit == 1:
            self.wait(reads, ("across", 1), bit, self.other, self.at.flip(1))
        elif bit == self.bits - 1:
            quad = jnp.logical_and(reads, jnp.logical_not(self.end()))
            self.wait(quad, ("quad", bit), bit, self.other, self.at.flip(1))
            self.wait(self.end(), ("diag", bit), bit, self.other, self.at.aslant(bit))
        else:
            self.wait(reads, ("quad", bit), bit, self.other, self.at.flip(1))
        self.forward(reads, ("far", bit), bit, self.other, self.at.mate)

    def finish(self, bit):
        self.wait(self.reads(bit), ("near", bit), bit, self.mate_head, self.at.mate)
        self.wait(self.reads(bit), ("far", bit), bit, self.mate_other, self.at.mate)

    def drain(self):
        for when, args in self.sent:
            guarded(when, lambda: self.copy(*args).wait_send())


def guarded(when, fn):
    if when is None:
        fn()
    else:
        pl.when(when)(fn)


def product(a, b, dims):
    return lax.dot_general(a, b, (dims, ((), ())), preferred_element_type=jnp.float32)


def head_cols(h):
    return pl.ds(h * HEAD, HEAD)


def layer_kernel(
    groups, seqs, tokens_hbm, w_ref, wo_ref, lw_hbm, out_ref,
    tokens_ref, kv_buf, q_buf, wo_buf, total, qkv, mix, acc, attended, lw_ref, flat, weight_ref, local_sum, first_sum, give, pair,
    pair_give, run_give, left, load_sem, kv_send, kv_recv, q_send, q_recv, wo_send, wo_recv, ex_send, ex_recv,
):
    place = Place(groups, seqs)
    rows_w, columns = w_ref.shape
    wide = HEADS * HEAD
    here = place.me
    loads = [
        pltpu.make_async_copy(src, dst, load_sem.at[n])
        for n, (src, dst) in enumerate(
            (
                (w_ref.at[:, pl.ds(wide, columns - wide)], kv_buf.at[here]),
                (w_ref.at[:, pl.ds(0, wide)], q_buf.at[here]),
                (wo_ref, wo_buf.at[here]),
                (lw_hbm, lw_ref),
                (tokens_hbm, tokens_ref),
            )
        )
    ]
    for one in loads:
        one.start()
    seq_bits = seqs.bit_length() - 1
    place.greet(place.neighbours() + [place.flip(b) for b in range(1, seq_bits)] + [place.aslant(seq_bits - 1)])
    kv = Gather(place, kv_buf, PIECES[0], SHARE[0], kv_send, kv_recv)
    q = Gather(place, q_buf, PIECES[1], SHARE[1], q_send, q_recv)
    wo = Gather(place, wo_buf, PIECES[2], SHARE[2], wo_send, wo_recv)
    streams = (kv, q, wo)
    last = kv.last
    loads[0].wait()
    kv.begin_all()
    kv.own()
    for one in loads[1:]:
        one.wait()
    for stream in streams[1:]:
        stream.own()

    count = tokens_ref.shape[0] // SPAN
    levels, heads, tokens_here = lw_ref.shape

    for level in range(levels):
        flat[level * heads : (level + 1) * heads, :] = lw_ref[level]
    spare = flat.shape[0] - levels * heads
    if spare:
        flat[levels * heads :, :] = jnp.zeros((spare, tokens_here), jnp.float32)
    weight_ref[...] = flat[...].T

    def mixing(c, h):
        rows = pl.ds(c * SPAN, SPAN)
        i = lax.broadcasted_iota(jnp.int32, (SPAN, SPAN), 0)
        j = lax.broadcasted_iota(jnp.int32, (SPAN, SPAN), 1)
        apart = i ^ j
        value = jnp.zeros((SPAN, SPAN), jnp.float32)
        for level in range(CBITS + 1):
            gain = 1.0 / math.sqrt(HEAD * max(1, 2 ** (level - 1)))
            column = weight_ref[rows, level * HEADS + h : level * HEADS + h + 1] * gain
            column = jnp.broadcast_to(column, (SPAN, SPAN))
            value = column if level == 0 else jnp.where(apart >= 2 ** (level - 1), column, value)
        mix[c, h] = jnp.where(i >= j, value, 0.0)

    aligned = (2 * rows_w) % 128 == 0

    def use(stream, base, step, tile):
        if not aligned:
            return
        cols = pl.ds(tile * TILE, TILE)
        y = None
        for offset in stream.offsets(step):
            chip = place.chip_at(offset)
            x = tokens_ref[:, pl.ds(pl.multiple_of(chip * (2 * rows_w), 128), 2 * rows_w)]
            w = stream.buf[pl.ds(chip * 2, 2), :, cols].reshape(2 * rows_w, TILE)
            part = jnp.dot(x, w, preferred_element_type=jnp.float32)
            y = part if y is None else y + part
        if step:
            y = total[:, pl.ds(base + tile * TILE, TILE)] + y
        if step < last:
            total[:, pl.ds(base + tile * TILE, TILE)] = y
        else:
            qkv[:, pl.ds(base + tile * TILE, TILE)] = y.astype(qkv.dtype)

    def at_once(stream, base):
        if aligned:
            return

        @pl.loop(0, stream.columns // TILE)
        def _(t):
            cols = pl.ds(pl.multiple_of(t * TILE, TILE), TILE)
            w = stream.buf[:, :, cols].reshape(seqs * rows_w, TILE)
            y = jnp.dot(tokens_ref[...], w, preferred_element_type=jnp.float32)
            qkv[:, pl.ds(pl.multiple_of(base + t * TILE, TILE), TILE)] = y.astype(qkv.dtype)

    exchange = Exchange(place, left, seq_bits, ex_send, ex_recv)

    def states(h):
        for c in range(count):
            k = qkv[pl.ds(c * SPAN, SPAN), head_cols(HEADS + h)]
            v = qkv[pl.ds(c * SPAN, SPAN), head_cols(2 * HEADS + h)]
            state = product(k, v, ((0,), (0,)))
            if c == 0:
                local_sum[h] = state
                first_sum[h] = state.astype(jnp.bfloat16)
            else:
                local_sum[h] += state
        give[h] = local_sum[h].astype(jnp.bfloat16)
        exchange.send(None, ("core", h), give.at[h], 0, h, place.mate)

    running = {}

    def exchange_core():
        for h in range(HEADS):
            exchange.wait(None, ("core", h), 0, h, place.mate)
        for n in range(2):
            h = 2 * place.core + n
            pair[n] = local_sum[h] + left[0, h].astype(jnp.float32)
            pair_give[n] = pair[n].astype(jnp.bfloat16)
        y = place.digit(1)
        for n, which in enumerate((1 - y, y)):
            exchange.send(y == 0 if n else None, ("across", n), pair_give.at[which], 1, 2 * place.core + which, place.flip(1))

    def exchange_across():
        y = place.digit(1)
        exchange.wait(None, ("across", 0), 1, exchange.head, place.flip(1))
        pair[0] = pair[y] + left[1, exchange.head].astype(jnp.float32)
        run_give[2] = pair[0].astype(jnp.bfloat16)
        exchange.hop(2, run_give.at[2])
        exchange.spread(1)

    def exchange_hop(bit):
        exchange.hopped(bit)
        if bit + 1 < seq_bits:
            pair[0] += left[bit, exchange.head].astype(jnp.float32)
            run_give[bit + 1] = pair[0].astype(jnp.bfloat16)
            exchange.hop(bit + 1, run_give.at[bit + 1])
        exchange.spread(bit)

    local_bits = count.bit_length() - 1

    def gain_of(level):
        return 1.0 / math.sqrt(SPAN * 2 ** (level - 1) * HEAD)

    def weight_of(rows, level, h):
        at = (CBITS + level) * HEADS + h
        return weight_ref[rows, at : at + 1]

    def attend(c, h):
        rows = pl.ds(c * SPAN, SPAN)
        qs = qkv[rows, head_cols(h)]
        k = qkv[rows, head_cols(HEADS + h)]
        v = qkv[rows, head_cols(2 * HEADS + h)]
        scores = product(qs, k, ((1,), (1,)))
        probs = (scores * mix[c, h]).astype(jnp.bfloat16)
        got = product(probs, v, ((1,), (0,)))
        if c > 0:
            got += product(qs, first_sum[h], ((1,), (0,))) * (weight_of(rows, 1, h) * gain_of(1))
        acc[rows, head_cols(h)] = got

    def read(h):
        rows = pl.ds(0, count * SPAN)
        qs = qkv[:, head_cols(h)]
        got = acc[:, head_cols(h)]
        for bit in range(seq_bits):
            level = local_bits + bit + 1
            part = product(qs, left[bit, h], ((1,), (0,))) * (weight_of(rows, level, h) * gain_of(level))
            got += jnp.where(place.digit(bit) == 1, part, 0.0)
        attended[:, head_cols(h)] = got.astype(jnp.bfloat16)

    def project(near, tile):
        cols = pl.ds(tile * TILE, TILE)
        half = here // (seqs // 2)
        half = half if near else 1 - half
        deep = seqs // 2 * wo.rows
        w = wo_buf[pl.ds(half * (seqs // 2), seqs // 2), :, cols].reshape(deep, TILE)
        x = attended[:, pl.ds(pl.multiple_of(half * deep, 128), deep)]
        y = jnp.dot(x, w, preferred_element_type=jnp.float32)
        if near:
            total[:, cols] = y
        else:
            out_ref[:, cols] = (total[:, cols] + y).astype(out_ref.dtype)

    order = [(0, step) for step in range(1, last + 1)]
    split = max(last - APART, 0)
    order += [(n, step) for step in range(1, split + 1) for n in (1, 2)]
    order += [(n, step) for n in (1, 2) for step in range(split + 1, last + 1)]
    plan, end = [], {}
    for n, step in order:
        plan += [(n, step, group) for group in streams[n].groups(step)]
        end[n, step] = len(plan) - 1
    items = []

    def add(ready, cost, fn, *args):
        items.append((ready, cost, functools.partial(fn, *args)))

    for c in range(count):
        for h in range(HEADS):
            add(0, 1, mixing, c, h)
    done = {}
    for n, stream in enumerate(streams):
        for step in range(last + 1):
            done[n, step] = end[n, step] + LAG[n] + CLAG[n] if step else (end[0, last] + 1 if n else 0)
    ex_items = []

    def flush():
        while ex_items:
            ex_items.pop(0)[1]()

    for n, base in ((0, wide), (1, 0)):
        for step in range(last + 1):
            add(done[n, step], 0, streams[n].complete, step)
            for tile in range(streams[n].columns // TILE):
                add(done[n, step], 2 if streams[n].offsets(step)[1:] else 1, use, streams[n], base, step, tile)
        add(done[n, last], 0, at_once, streams[n], base)
        for h in range(HEADS) if n == 0 else ():
            add(done[n, last], 1, states, h)
    for h in range(HEADS):
        for c in range(count):
            add(done[1, last], 1, attend, c, h)
    for step in range(last + 1):
        add(done[2, step], 0, wo.complete, step)
    add(min(done[0, last] + 8, len(plan) - 1), 0, kv.drain)
    for stream in (q, wo):
        add(len(plan) - 1, 0, stream.drain, (last - 1, last))
    items.sort(key=lambda item: item[0])

    steps = [exchange_core, exchange_across] + [functools.partial(exchange_hop, b) for b in range(2, seq_bits)]
    at = done[0, last] + EX_FIRST
    for n, fn in enumerate(steps):
        ex_items.append((at + n * EX_LAG, fn))
        if n > 1:
            ex_items.append((at + n * EX_LAG + 1, functools.partial(exchange.collect, n - 1)))
    ex_items.append((at + (len(steps) - 1) * EX_LAG + 3, functools.partial(exchange.collect, seq_bits - 1)))
    for bit in range(1, seq_bits):
        ex_items.append((at + (len(steps) - 1) * EX_LAG + 5, functools.partial(exchange.finish, bit)))

    settles = {}
    for n, stream in enumerate(streams):
        for step in range(1, last + 1):
            settles.setdefault(end[n, step] + LAG[n], []).append(functools.partial(stream.settle, step))

    def run(tick, budget):
        for fn in settles.pop(tick, ()):
            fn()
        while ex_items and ex_items[0][0] <= tick and tick < len(plan):
            ready_at, fn = ex_items[0]
            if any(item[2].func is states or item[2].func is use and item[2].args[0] is kv for item in items):
                break
            ex_items.pop(0)
            fn()
        spent = 0
        while items and items[0][0] <= tick and (spent == 0 or spent + items[0][1] <= budget):
            _, cost, fn = items.pop(0)
            fn()
            spent += cost

    run(0, BEFORE)
    for tick, (n, step, group) in enumerate(plan):
        behind = (None if split else wo) if n else q
        for h, d in group:
            streams[n].arrive(step, h, d, behind)
        if tick == end[0, last]:
            q.begin_all()
            if split:
                wo.begin_all()
        if tick == end[1, last]:
            wo.begin_all()
        run(tick, BUDGET[n])
    late = sorted(settles)
    for tick in late[:-1]:
        for fn in settles[tick]:
            fn()
    tail = [fn for _, _, fn in items]
    ends = [fn for fn in tail if fn.func == wo.complete]
    for fn in tail:
        if fn not in ends:
            fn()
    for fn in settles[late[-1]] if late else ():
        fn()
    flush()
    for h in range(HEADS):
        read(h)
    tiles = range(wo.columns // TILE)
    for fn in ends[:-1]:
        fn()
    for tile in tiles:
        project(True, tile)
    ends[-1]()
    for tile in tiles:
        project(False, tile)
    for one in (*streams, exchange):
        one.drain()


def on_device(tokens, w_qkv, w_out, level_weight):
    groups, seqs = lax.axis_size("group"), lax.axis_size("seq")
    rows = tokens.shape[0]
    count = rows // SPAN
    seq_bits = seqs.bit_length() - 1
    wide = HEADS * HEAD
    square = (HEAD, HEAD)
    flat_rows = -(-level_weight.shape[0] * level_weight.shape[1] // 8) * 8
    vmem = pl.BlockSpec(memory_space=pltpu.VMEM)
    hbm = pl.BlockSpec(memory_space=pl.ANY)
    sems = pltpu.SemaphoreType.DMA((slots_needed(seqs),))
    return pl.pallas_call(
        functools.partial(layer_kernel, groups, seqs),
        out_shape=pltpu.VMEM((rows, w_out.shape[1]), jnp.bfloat16),
        in_specs=[hbm, hbm, hbm, hbm],
        out_specs=vmem,
        scratch_shapes=[
            pltpu.VMEM(tokens.shape, jnp.bfloat16),
            pltpu.VMEM((seqs, w_qkv.shape[0], 2 * wide), jnp.bfloat16),
            pltpu.VMEM((seqs, w_qkv.shape[0], wide), jnp.bfloat16),
            pltpu.VMEM((seqs, *w_out.shape), jnp.bfloat16),
            pltpu.VMEM((rows, w_qkv.shape[1]), jnp.float32),
            pltpu.VMEM((rows, w_qkv.shape[1]), jnp.bfloat16),
            pltpu.VMEM((count, HEADS, SPAN, SPAN), jnp.float32),
            pltpu.VMEM((rows, wide), jnp.float32),
            pltpu.VMEM((rows, wide), jnp.bfloat16),
            pltpu.VMEM(level_weight.shape, jnp.float32),
            pltpu.VMEM((flat_rows, rows), jnp.float32),
            pltpu.VMEM((rows, flat_rows), jnp.float32),
            pltpu.VMEM((HEADS, *square), jnp.float32),
            pltpu.VMEM((HEADS, *square), jnp.bfloat16),
            pltpu.VMEM((HEADS, *square), jnp.bfloat16),
            pltpu.VMEM((2, *square), jnp.float32),
            pltpu.VMEM((2, *square), jnp.bfloat16),
            pltpu.VMEM((seq_bits, *square), jnp.bfloat16),
            pltpu.VMEM((seq_bits, HEADS, *square), jnp.bfloat16),
            pltpu.SemaphoreType.DMA((5,)),
            *[sems] * 6,
            pltpu.SemaphoreType.DMA((8 * seq_bits,)),
            pltpu.SemaphoreType.DMA((8 * seq_bits,)),
        ],
        compiler_params=pltpu.CompilerParams(
            collective_id=0, has_side_effects=True, vmem_limit_bytes=58 * 1024 * 1024
        ),
    )(tokens, w_qkv, w_out, level_weight)


def solution(mesh):
    return jax.shard_map(
        on_device,
        mesh=mesh,
        in_specs=(
            P(("group", "seq"), None),
            P("seq", None),
            P("seq", None),
            P(None, None, ("group", "seq")),
        ),
        out_specs=P(("group", "seq"), None),
        check_vma=False,
    )
```
